128 devices in a mesh: section: 16 (over z_lo, x, core), tensor: 8 (over z_hi, y).
Axes of the slice: x: 4, y: 4, z: 4 (z_hi: 2, z_lo: 2; z = z_hi * 2 + z_lo), core: 2. Of those that a mesh axis runs over, the one named last changes fastest.
Arguments:
- matching: int32 [16], replicated, may hold values from 0 to 15, each once
- lengths: int32 [32], replicated, may hold values from 2 to 255
- queries: bfloat16 [16, 32, 8192], P('section', None, 'tensor'), may hold values from -200 to 200
- kv_cache: bfloat16 [16, 32, 256, 2048], P('section', None, None, 'tensor'), may hold values from -6 to 6
- incoming_key_value: bfloat16 [16, 32, 2048], P('section', None, 'tensor'), may hold values from -6 to 6
- residual: bfloat16 [16, 32, 8192], P('section', None, 'tensor'), may hold values from -6 to 6
- out_weight: bfloat16 [16, 8192, 8192], P('section', 'tensor'), may hold values from -0.09375 to 0.09375
- norm_gain: bfloat16 [16, 8192], P('section', 'tensor'), may hold values from 0.5 to 1.5
Outputs:
- cache_out: bfloat16 [16, 32, 256, 2048], P('section', None, None, 'tensor')
- stream_out: bfloat16 [16, 32, 8192], P('section', None, 'tensor')
- normed_out: bfloat16 [16, 32, 8192], P('section', None, 'tensor')
The draws below stay inside these ranges and needn't reach their ends.
All inputs are finite; a program needn't handle non-finite values.
Results may differ from the reference program's by a relative error of at most 0.0042.
Values may be sent and summed in bfloat16 or wider, within the bound.
A program may use at most 128 MiB of HBM per device.

```python
import math
import jax
import jax.numpy as jnp
from jax import lax

D = 8192
QUERY_HEADS = 64
KEY_VALUE_HEADS = 8
HEAD_SIZE = 128
BATCH_SEQUENCES = 32
CONTEXT_SLOTS = 256
LAYER_COUNT = 16
QUERY_PER_KEY = 8
N_SECTION = 16


def leading_keys(key):
    return jnp.clip(jax.random.normal(jax.random.fold_in(key, 11), (LAYER_COUNT, BATCH_SEQUENCES, 2, KEY_VALUE_HEADS * 2 * HEAD_SIZE), jnp.float32), -6.0, 6.0)


def draw_kv_cache(key, part):
    slots_per_head = leading_keys(key)
    remaining_slots = jnp.clip(jax.random.normal(jax.random.fold_in(key, 12), (LAYER_COUNT, BATCH_SEQUENCES, CONTEXT_SLOTS - 2, KEY_VALUE_HEADS * 2 * HEAD_SIZE), jnp.float32), -6.0, 6.0)
    return jnp.concatenate([slots_per_head, remaining_slots], axis=2).astype(jnp.bfloat16)


def draw_queries(key, part):
    base = jnp.clip(jax.random.normal(jax.random.fold_in(key, 13), (LAYER_COUNT, BATCH_SEQUENCES, QUERY_HEADS * HEAD_SIZE), jnp.float32), -6.0, 6.0)
    return base.astype(jnp.bfloat16)


def set_ends(result, rng, low, largest):
    extent = result.shape
    spot = [jax.random.randint(jax.random.fold_in(rng, axis), (), 0, extent[axis]) for axis in range(len(extent))]
    result = result.at[tuple(spot)].set(low)
    longest = extent.index(max(extent))
    spot[longest] = (spot[longest] + 1) % extent[longest]
    return result.at[tuple(spot)].set(largest)


def raised(result, stream_key, source, target, parts, factor):
    owner, partner = [(jnp.arange(result.shape[axis_at]) // (result.shape[axis_at] // parts)).reshape([-1 if axis == axis_at else 1 for axis in range(result.ndim)]) for axis_at in (source, target)]
    chosen = jax.random.permutation(stream_key, parts)[partner]
    strong = (owner == chosen) | (owner == (partner + parts // 2) % parts)
    return jnp.where(strong, factor * result, result)


def shard_levels(key, dims, pieces, smallest, high):
    factor_of = 1.0
    for axis_at, shards_of in pieces:
        draws = jax.random.uniform(jax.random.fold_in(jax.random.fold_in(key, 6), axis_at), (shards_of,), jnp.float32, smallest / len(pieces), high / len(pieces))
        factor_of = factor_of * jnp.repeat(jnp.exp(draws), dims[axis_at] // shards_of).reshape((-1,) + (1,) * (len(dims) - 1 - axis_at))
    return factor_of


def noise(rng, extent, width, most, pieces=(), held_as=jnp.bfloat16):
    entries = width * jax.random.normal(rng, extent, jnp.float32)
    if pieces:
        entries = entries * shard_levels(rng, extent, pieces, -0.22, 0.18)
    return jnp.clip(entries, -most, most).astype(held_as)


def noise_with(key, extent, scale, most, split, heavy, kind=jnp.bfloat16):
    values = scale * jax.random.normal(key, extent, jnp.float32)
    if split:
        values = values * shard_levels(key, extent, split, -0.22, 0.18)
    return jnp.clip(raised(values, jax.random.fold_in(key, 3), *heavy), -most, most).astype(kind)


def setup_inputs(seed: int = 0) -> dict:
    splits = jax.random.split(jax.random.key(seed), 9)
    matching = jax.random.permutation(splits[0], N_SECTION).astype(jnp.int32)
    lengths = set_ends(jax.random.randint(splits[1], (BATCH_SEQUENCES,), 2, CONTEXT_SLOTS), jax.random.fold_in(splits[1], 1), 2, CONTEXT_SLOTS - 1).astype(jnp.int32)
    queries = draw_queries(jax.random.fold_in(splits[8], 71), 0)
    kv_cache = draw_kv_cache(jax.random.fold_in(splits[8], 71), 0)
    incoming_key_value = noise(splits[4], (LAYER_COUNT, BATCH_SEQUENCES, KEY_VALUE_HEADS * 2 * HEAD_SIZE), 1.0, 6.0, ((0, 16), (2, 8)))
    residual = noise(splits[5], (LAYER_COUNT, BATCH_SEQUENCES, D), 1.0, 6.0, ((0, 16), (2, 8)))
    out_weight = noise_with(splits[6], (LAYER_COUNT, QUERY_HEADS * HEAD_SIZE, D), (QUERY_HEADS * HEAD_SIZE) ** -0.5, 0.09375, ((0, 16), (1, 8)), (1, 2, 8, 2.0))
    norm_gain = jnp.clip(1.0 + 0.1 * jax.random.normal(splits[7], (LAYER_COUNT, D), jnp.float32), 0.5, 1.5).astype(jnp.bfloat16)
    return {"matching": matching, "lengths": lengths, "queries": queries, "kv_cache": kv_cache, "incoming_key_value": incoming_key_value, "residual": residual, "out_weight": out_weight, "norm_gain": norm_gain}


def layer_step(query_vectors, cache_rows, fresh_rows, residual_rows, projection, gain_row, lengths):
    places = jnp.arange(CONTEXT_SLOTS, dtype=jnp.int32)
    written = places[None, :] == lengths[:, None]
    updated_cache = jnp.where(written[:, :, None], fresh_rows[:, None, :], cache_rows)
    heads_separated = updated_cache.reshape(BATCH_SEQUENCES, CONTEXT_SLOTS, KEY_VALUE_HEADS, 2, HEAD_SIZE)
    key_rows = heads_separated[:, :, :, 0].astype(jnp.float32)
    value_rows = heads_separated[:, :, :, 1].astype(jnp.float32)
    grouped_queries = query_vectors.reshape(BATCH_SEQUENCES, KEY_VALUE_HEADS, QUERY_PER_KEY, HEAD_SIZE).astype(jnp.float32)
    scores = jnp.einsum('bgrd,bsgd->bgrs', grouped_queries, key_rows) / math.sqrt(HEAD_SIZE)
    visible = places[None, :] <= lengths[:, None]
    scores = jnp.where(visible[:, None, None, :], scores, -1e+30)
    weights = jax.nn.softmax(scores, axis=-1).astype(jnp.bfloat16)
    attended = jnp.einsum('bgrs,bsgd->bgrd', weights.astype(jnp.float32), value_rows).astype(jnp.bfloat16)
    partial_value = jnp.dot(attended.reshape(BATCH_SEQUENCES, QUERY_HEADS * HEAD_SIZE), projection, preferred_element_type=jnp.float32)
    stream = residual_rows.astype(jnp.float32) + partial_value
    scale = lax.rsqrt(lax.optimization_barrier(jnp.mean(stream * stream, axis=-1, keepdims=True)) + 1e-05)
    normed = stream * scale * gain_row.astype(jnp.float32)
    return (updated_cache, stream.astype(jnp.bfloat16), normed.astype(jnp.bfloat16))

def reference(matching, lengths, queries, kv_cache, incoming_key_value, residual, out_weight, norm_gain):

    def one_layer(layer_idx):
        return layer_step(queries[layer_idx], kv_cache[layer_idx], incoming_key_value[layer_idx], residual[layer_idx], out_weight[layer_idx], norm_gain[layer_idx], lengths)
    cache_out, stream_out, normed_out = lax.map(one_layer, matching)
    return (cache_out, stream_out, normed_out)
```

```python
import functools
import math

import jax
import jax.numpy as jnp
from jax import lax
from jax.experimental import pallas as pl
from jax.experimental.pallas import tpu as pltpu
from jax.sharding import PartitionSpec as P

MESH = pl.DeviceIdType.MESH
D = 8192
HEAD = 128
BATCH = 32
SLOTS = 256
GROUPS = 16
CHUNKS = 4
PER_CHUNK = SLOTS // CHUNKS
F32 = jnp.float32
BF16 = jnp.bfloat16

OFFSETS = []
for other_core in (0, 1):
    OFFSETS += [
        (1, 2, other_core), (0, 1, other_core), (1, 3, other_core), (0, 2, other_core),
        (1, 1, other_core), (0, 3, other_core), (1, 0, other_core),
    ]
OFFSETS += [(0, 0, 1)]
PARTNERS = len(OFFSETS)


def kernel(
    matching, lengths, queries, kv, fresh, residual, weight, gain,
    cache_out, stream_out, normed_out,
    cache, fresh32, attended, wide, partial, y_got, z_part, z_got, squares, sq_y, sq_z, sq_zs,
    mine, rows_got, rows_next, rows_last, got, nxt,
    load_sem, weight_sem, send1, recv1, send2, recv2, own_sem,
    y_send, y_recv, z_send, z_recv, sy_send, sy_recv, sz_send, sz_recv,
    rs1, rr1, rs2, rr2,
):
    me = lax.axis_index("section")
    zlo, x, core = me // 8, (me // 2) % 4, me % 2
    t = lax.axis_index("tensor")
    zhi, y = t // 4, t % 4
    partners = [
        ((zlo + dz) % 2) * 8 + ((x + dx) % 4) * 2 + (core + dc) % 2 for dz, dx, dc in OFFSETS
    ]
    y_partners = [zhi * 4 + (y + d) % 4 for d in (1, 2, 3)]
    z_partner = (1 - zhi) * 4 + y

    def to(src, dst, ss, rs, **where):
        return pltpu.make_async_remote_copy(
            src, dst, ss, rs, device_id=where, device_id_type=MESH
        )

    def load(q):
        rows = pl.ds(q * PER_CHUNK, PER_CHUNK)
        return pltpu.make_async_copy(kv.at[:, rows], cache.at[:, rows], load_sem.at[q])

    for q in range(CHUNKS):
        load(q).start()

    def block_of(n):
        return (n % 2) * 4 + (y + 1 + n // 2) % 4

    def load_weight(n):
        cols = pl.ds(pl.multiple_of(block_of(n) * 1024, 1024), 1024)
        return pltpu.make_async_copy(weight.at[:, cols], wide.at[n], weight_sem.at[n])

    for n in range(8):
        load_weight(n).start()

    barrier = pltpu.get_barrier_semaphore()
    for p in partners:
        pl.semaphore_signal(barrier, inc=1, device_id={"section": p}, device_id_type=MESH)
    for p in y_partners + [z_partner]:
        pl.semaphore_signal(barrier, inc=1, device_id={"tensor": p}, device_id_type=MESH)

    fresh32[...] = fresh[...].astype(F32)

    def spread(q, k):
        p = partners[k]
        return to(
            cache.at[pl.ds(2 * p, 2), pl.ds(q * PER_CHUNK, PER_CHUNK)], got[q].at[me],
            send1.at[q, k], recv1.at[q, k], section=p,
        )

    def keep(q):
        return pltpu.make_async_copy(
            cache.at[pl.ds(2 * me, 2), pl.ds(q * PER_CHUNK, PER_CHUNK)], got[q].at[me],
            own_sem.at[0, q],
        )

    for q in range(CHUNKS):
        load(q).wait()

        def write(b, _):
            rows = pl.ds(q * PER_CHUNK, PER_CHUNK)
            old = cache[b, rows, :].astype(F32)
            place = lax.broadcasted_iota(jnp.int32, (PER_CHUNK, 2 * HEAD), 0) + q * PER_CHUNK
            new = jnp.broadcast_to(fresh32[pl.ds(b, 1), :], old.shape)
            cache[b, rows, :] = jnp.where(place == lengths[b], new, old).astype(BF16)
            return 0

        lax.fori_loop(0, BATCH, write, 0)
        if q == 0:
            pl.semaphore_wait(barrier, PARTNERS + 4)
        for k in range(PARTNERS):
            spread(q, k).start()
        keep(q).start()

    def attend(b, _):
        keys, values = cache[b, :, :HEAD], cache[b, :, HEAD:]
        scores = lax.dot_general(
            queries[b], keys, (((1,), (1,)), ((), ())), preferred_element_type=F32
        ) * (1.0 / math.sqrt(HEAD))
        place = lax.broadcasted_iota(jnp.int32, scores.shape, 1)
        scores = jnp.where(place <= lengths[b], scores, -1e30)
        grown = jnp.exp(scores - jnp.max(scores, axis=1, keepdims=True))
        weights = (grown / jnp.sum(grown, axis=1, keepdims=True)).astype(BF16)
        result = jnp.dot(weights, values, preferred_element_type=F32)
        attended[pl.ds(pl.multiple_of(b * 8, 8), 8), :] = result.astype(BF16).astype(F32)
        return 0

    lax.fori_loop(0, BATCH, attend, 0)
    heads = jnp.concatenate(
        [attended[pl.ds(h, BATCH, stride=8), :].astype(BF16) for h in range(8)], axis=1
    )

    def y_part(i, z2):
        return to(
            partial.at[z2 * 4 + (y + 1 + i) % 4], y_got.at[i, z2],
            y_send.at[i, z2], y_recv.at[i, z2], tensor=y_partners[i],
        )

    for n in range(8):
        load_weight(n).wait()
        partial[block_of(n)] = jnp.dot(heads, wide[n], preferred_element_type=F32)
        if n < 6:
            y_part(n // 2, n % 2).start()

    def pass_on(q):
        return [
            to(
                nxt[q].at[partners[k]],
                cache_out.at[pl.ds(2 * me, 2), pl.ds(q * PER_CHUNK, PER_CHUNK)],
                send2.at[q, k], recv2.at[q, k], section=partners[k],
            )
            for k in range(PARTNERS)
        ]

    def leave(q):
        return pltpu.make_async_copy(
            nxt[q].at[me], cache_out.at[pl.ds(2 * me, 2), pl.ds(q * PER_CHUNK, PER_CHUNK)],
            own_sem.at[1, q],
        )

    def turn(q):
        keep(q).wait()
        for k in range(PARTNERS):
            spread(q, k).wait_recv()

        def pick(p, _):
            nxt[q][p] = got[q][matching[p]]
            return 0

        lax.fori_loop(0, GROUPS, pick, 0)
        for copy in pass_on(q):
            copy.start()
        leave(q).start()

    for i in range(3):
        for z2 in range(2):
            y_part(i, z2).wait_recv()
    z_part[...] = partial[(1 - zhi) * 4 + y] + (
        y_got[0, 1 - zhi] + y_got[1, 1 - zhi] + y_got[2, 1 - zhi]
    )
    z_copy = to(z_part, z_got, z_send, z_recv, tensor=z_partner)
    z_copy.start()
    stream = partial[zhi * 4 + y] + (y_got[0, zhi] + y_got[1, zhi] + y_got[2, zhi])
    z_copy.wait_recv()
    stream = stream + z_got[...] + residual[...].astype(F32)
    squares[...] = jnp.broadcast_to(
        jnp.sum(stream * stream, axis=1, keepdims=True), squares.shape
    )
    sq_copies = [
        to(squares, sq_y.at[i], sy_send.at[i], sy_recv.at[i], tensor=y_partners[i])
        for i in range(3)
    ]
    for copy in sq_copies:
        copy.start()
    for copy in sq_copies:
        copy.wait_recv()
    sq_zs[...] = squares[...] + (sq_y[0] + sq_y[1] + sq_y[2])
    sq_copy = to(sq_zs, sq_z, sz_send, sz_recv, tensor=z_partner)
    sq_copy.start()
    sq_copy.wait_recv()
    scale = lax.rsqrt((sq_zs[:, :1] + sq_z[:, :1]) / D + 1e-05)
    normed = (stream * scale * gain[...].astype(F32)).astype(BF16)
    stream = stream.astype(BF16)
    for j in range(GROUPS):
        r, c = (j // 8) * 16, (j % 8) * HEAD
        mine[j, 0] = stream[r : r + 16, c : c + HEAD]
        mine[j, 1] = normed[r : r + 16, c : c + HEAD]
    row_copies = [
        to(mine.at[p], rows_got.at[me], rs1.at[k], rr1.at[k], section=p)
        for k, p in enumerate(partners)
    ]
    for copy in row_copies:
        copy.start()
    rows_got[me] = mine[me]

    for q in range(CHUNKS - 1):
        turn(q)

    for copy in row_copies:
        copy.wait_recv()

    def pick_rows(p, _):
        rows_next[p] = rows_got[matching[p]]
        return 0

    lax.fori_loop(0, GROUPS, pick_rows, 0)
    row_copies2 = [
        to(rows_next.at[p], rows_last.at[me], rs2.at[k], rr2.at[k], section=p)
        for k, p in enumerate(partners)
    ]
    for copy in row_copies2:
        copy.start()
    rows_last[me] = rows_next[me]

    turn(CHUNKS - 1)

    for copy in row_copies2:
        copy.wait_recv()
    for j in range(GROUPS):
        r, c = (j // 8) * 16, (j % 8) * HEAD
        stream_out[r : r + 16, c : c + HEAD] = rows_last[j, 0]
        normed_out[r : r + 16, c : c + HEAD] = rows_last[j, 1]

    for i in range(3):
        for z2 in range(2):
            y_part(i, z2).wait_send()
    z_copy.wait_send()
    sq_copy.wait_send()
    for copy in sq_copies + row_copies + row_copies2:
        copy.wait_send()
    for q in range(CHUNKS):
        for k in range(PARTNERS):
            spread(q, k).wait_send()
    for q in range(CHUNKS):
        for copy in pass_on(q):
            copy.wait()
        leave(q).wait()


def on_device(
    matching, lengths, queries, kv_cache, incoming_key_value, residual, out_weight, norm_gain
):
    smem = pl.BlockSpec(memory_space=pltpu.SMEM)
    vmem = pl.BlockSpec(memory_space=pltpu.VMEM)
    anywhere = pl.BlockSpec(memory_space=pl.ANY)
    chunk = pltpu.VMEM((GROUPS, 2, PER_CHUNK, 2 * HEAD), BF16)
    rows = pltpu.VMEM((GROUPS, 2, 16, HEAD), BF16)
    dma = pltpu.SemaphoreType.DMA
    cache_out, stream_out, normed_out = pl.pallas_call(
        kernel,
        out_shape=(
            jax.ShapeDtypeStruct((BATCH, SLOTS, 2 * HEAD), BF16),
            jax.ShapeDtypeStruct((BATCH, 1024), BF16),
            jax.ShapeDtypeStruct((BATCH, 1024), BF16),
        ),
        in_specs=[smem, smem, vmem, anywhere, vmem, vmem, anywhere, vmem],
        out_specs=(anywhere, vmem, vmem),
        scratch_shapes=[
            pltpu.VMEM((BATCH, SLOTS, 2 * HEAD), BF16),
            pltpu.VMEM((BATCH, 2 * HEAD), F32),
            pltpu.VMEM((BATCH * 8, HEAD), F32),
            pltpu.VMEM((8, 1024, 1024), BF16),
            pltpu.VMEM((8, BATCH, 1024), F32),
            pltpu.VMEM((3, 2, BATCH, 1024), F32),
            pltpu.VMEM((BATCH, 1024), F32),
            pltpu.VMEM((BATCH, 1024), F32),
            pltpu.VMEM((BATCH, HEAD), F32),
            pltpu.VMEM((3, BATCH, HEAD), F32),
            pltpu.VMEM((BATCH, HEAD), F32),
            pltpu.VMEM((BATCH, HEAD), F32),
            rows, rows, rows, rows,
            [chunk] * CHUNKS,
            [chunk] * CHUNKS,
            dma((CHUNKS,)), dma((8,)),
            dma((CHUNKS, PARTNERS)), dma((CHUNKS, PARTNERS)),
            dma((CHUNKS, PARTNERS)), dma((CHUNKS, PARTNERS)),
            dma((2, CHUNKS)),
            dma((3, 2)), dma((3, 2)), dma, dma,
            dma((3,)), dma((3,)), dma, dma,
            dma((PARTNERS,)), dma((PARTNERS,)), dma((PARTNERS,)), dma((PARTNERS,)),
        ],
        compiler_params=pltpu.CompilerParams(
            collective_id=0, has_side_effects=True, vmem_limit_bytes=56 << 20
        ),
    )(
        matching, lengths, queries.reshape(BATCH, 8, HEAD), kv_cache[0], incoming_key_value[0],
        residual[0], out_weight[0], norm_gain,
    )
    return cache_out[None], stream_out[None], normed_out[None]


def solution(mesh):
    return jax.shard_map(
        on_device,
        mesh=mesh,
        in_specs=(
            P(),
            P(),
            P("section", None, "tensor"),
            P("section", None, None, "tensor"),
            P("section", None, "tensor"),
            P("section", None, "tensor"),
            P("section", "tensor", None),
            P("section", "tensor"),
        ),
        out_specs=(
            P("section", None, None, "tensor"),
            P("section", None, "tensor"),
            P("section", None, "tensor"),
        ),
        check_vma=False,
    )
```

```python
import functools
import math

import jax
import jax.numpy as jnp
from jax import lax
from jax.experimental import pallas as pl
from jax.experimental.pallas import tpu as pltpu
from jax.sharding import PartitionSpec as P

MESH = pl.DeviceIdType.MESH
D = 8192
HEAD = 128
BATCH = 32
SLOTS = 256
GROUPS = 16
CHUNKS = 4
PER_CHUNK = SLOTS // CHUNKS
F32 = jnp.float32
BF16 = jnp.bfloat16

OFFSETS = []
for other_core in (0, 1):
    OFFSETS += [
        (1, 2, other_core), (0, 1, other_core), (1, 3, other_core), (0, 2, other_core),
        (1, 1, other_core), (0, 3, other_core), (1, 0, other_core),
    ]
OFFSETS += [(0, 0, 1)]
PARTNERS = len(OFFSETS)


def kernel(
    matching, lengths, queries, kv, fresh, residual, weight, gain,
    cache_out, rows_out,
    cache, fresh32, asked, attended, wide, partial, y_got, z_part, z_got, squares, sq_y, sq_z, sq_zs,
    mine, rows_got, rows_next, got, nxt,
    load_sem, weight_sem, send1, recv1, send2, recv2, own_sem,
    y_send, y_recv, z_send, z_recv, sy_send, sy_recv, sz_send, sz_recv,
    rs1, rr1, rs2, rr2,
):
    me = lax.axis_index("section")
    zlo, x, core = me // 8, (me // 2) % 4, me % 2
    t = lax.axis_index("tensor")
    zhi, y = t // 4, t % 4
    partners = [
        ((zlo + dz) % 2) * 8 + ((x + dx) % 4) * 2 + (core + dc) % 2 for dz, dx, dc in OFFSETS
    ]
    y_partners = [zhi * 4 + (y + d) % 4 for d in (1, 2, 3)]
    z_partner = (1 - zhi) * 4 + y

    def to(src, dst, ss, rs, **where):
        return pltpu.make_async_remote_copy(
            src, dst, ss, rs, device_id=where, device_id_type=MESH
        )

    barrier = pltpu.get_barrier_semaphore()
    for p in partners:
        pl.semaphore_signal(barrier, inc=1, device_id={"section": p}, device_id_type=MESH)
    for p in y_partners + [z_partner]:
        pl.semaphore_signal(barrier, inc=1, device_id={"tensor": p}, device_id_type=MESH)

    load = pltpu.make_async_copy(kv, cache, load_sem)
    load.start()

    def block_of(n):
        return (n % 2) * 4 + (y + 1 + n // 2) % 4

    def load_weight(n):
        cols = pl.ds(pl.multiple_of(block_of(n) * 1024, 1024), 1024)
        return pltpu.make_async_copy(weight.at[:, cols], wide.at[n], weight_sem.at[n])

    def spread(q, k):
        p = partners[k]
        return to(
            kv.at[pl.ds(2 * p, 2), pl.ds(q * PER_CHUNK, PER_CHUNK)], got[q].at[me],
            send1.at[q, k], recv1.at[q, k], section=p,
        )

    def keep(q):
        return pltpu.make_async_copy(
            kv.at[pl.ds(2 * me, 2), pl.ds(q * PER_CHUNK, PER_CHUNK)], got[q].at[me],
            own_sem.at[0, q],
        )

    def spread_all(q):
        for k in range(PARTNERS):
            spread(q, k).start()
        keep(q).start()

    pl.semaphore_wait(barrier, PARTNERS + 4)
    spread_all(0)
    for n in range(8):
        load_weight(n).start()
    for q in range(1, CHUNKS):
        spread_all(q)

    fresh32[...] = fresh[...].astype(F32)
    for h in range(8):
        asked[pl.ds(h, BATCH, stride=8), :] = queries[:, h * HEAD : (h + 1) * HEAD].astype(F32)
    load.wait()

    def attend(b):
        query = asked[pl.ds(pl.multiple_of(b * 8, 8), 8), :]
        keys, values = cache[b, :, :HEAD], cache[b, :, HEAD:]
        newest = fresh32[pl.ds(b, 1), :]
        new_key, new_value = newest[:, :HEAD], newest[:, HEAD:]
        scores = lax.dot_general(
            query.astype(BF16), keys, (((1,), (1,)), ((), ())), preferred_element_type=F32
        )
        place = lax.broadcasted_iota(jnp.int32, scores.shape, 1)
        own = jnp.sum(query * new_key, axis=1, keepdims=True)
        scores = jnp.where(place == lengths[b], own, scores) * (1.0 / math.sqrt(HEAD))
        scores = jnp.where(place <= lengths[b], scores, -1e30)
        grown = jnp.exp(scores - jnp.max(scores, axis=1, keepdims=True))
        weights = (grown / jnp.sum(grown, axis=1, keepdims=True)).astype(BF16).astype(F32)
        old = jnp.where(place == lengths[b], 0.0, weights)
        result = jnp.dot(old.astype(BF16), values, preferred_element_type=F32)
        result = result + jnp.sum(weights - old, axis=1, keepdims=True) * new_value
        attended[pl.ds(pl.multiple_of(b * 8, 8), 8), :] = result.astype(BF16).astype(F32)

    def attend_some(i, _):
        for j in range(4):
            attend(i * 4 + j)
        return 0

    lax.fori_loop(0, BATCH // 4, attend_some, 0)
    heads = jnp.concatenate(
        [attended[pl.ds(h, BATCH, stride=8), :].astype(BF16) for h in range(8)], axis=1
    )

    def y_part(i, z2):
        return to(
            partial.at[z2 * 4 + (y + 1 + i) % 4], y_got.at[i, z2],
            y_send.at[i, z2], y_recv.at[i, z2], tensor=y_partners[i],
        )

    for n in range(8):
        load_weight(n).wait()
        partial[block_of(n)] = jnp.dot(heads, wide[n], preferred_element_type=F32)
        if n < 6:
            y_part(n // 2, n % 2).start()

    def pass_on(q):
        return [
            to(
                nxt[q].at[partners[k]],
                cache_out.at[pl.ds(2 * me, 2), pl.ds(q * PER_CHUNK, PER_CHUNK)],
                send2.at[q, k], recv2.at[q, k], section=partners[k],
            )
            for k in range(PARTNERS)
        ]

    def leave(q):
        return pltpu.make_async_copy(
            nxt[q].at[me], cache_out.at[pl.ds(2 * me, 2), pl.ds(q * PER_CHUNK, PER_CHUNK)],
            own_sem.at[1, q],
        )

    def turn(q):
        keep(q).wait()
        for k in range(PARTNERS):
            spread(q, k).wait_recv()

        def pick(p, _):
            nxt[q][p] = got[q][matching[p]]
            return 0

        lax.fori_loop(0, GROUPS, pick, 0)
        for copy in pass_on(q):
            copy.start()
        leave(q).start()

    turn(0)
    for i in range(3):
        for z2 in range(2):
            y_part(i, z2).wait_recv()
    z_part[...] = partial[(1 - zhi) * 4 + y] + (
        y_got[0, 1 - zhi] + y_got[1, 1 - zhi] + y_got[2, 1 - zhi]
    )
    z_copy = to(z_part, z_got, z_send, z_recv, tensor=z_partner)
    z_copy.start()
    stream = partial[zhi * 4 + y] + (y_got[0, zhi] + y_got[1, zhi] + y_got[2, zhi])
    turn(1)
    z_copy.wait_recv()
    stream = stream + z_got[...] + residual[...].astype(F32)
    squares[...] = jnp.broadcast_to(
        jnp.sum(stream * stream, axis=1, keepdims=True), squares.shape
    )
    sq_copies = [
        to(squares, sq_y.at[i], sy_send.at[i], sy_recv.at[i], tensor=y_partners[i])
        for i in range(3)
    ]
    for copy in sq_copies:
        copy.start()
    for copy in sq_copies:
        copy.wait_recv()
    sq_zs[...] = squares[...] + (sq_y[0] + sq_y[1] + sq_y[2])
    sq_copy = to(sq_zs, sq_z, sz_send, sz_recv, tensor=z_partner)
    sq_copy.start()
    turn(2)
    sq_copy.wait_recv()
    scale = lax.rsqrt((sq_zs[:, :1] + sq_z[:, :1]) / D + 1e-05)
    normed = (stream * scale * gain[...].astype(F32)).astype(BF16)
    stream = stream.astype(BF16)
    filler = jnp.zeros((12, HEAD), F32)
    for j in range(GROUPS):
        r, c = (j // 8) * 16, (j % 8) * HEAD
        mine[j, 0] = stream[r : r + 16, c : c + HEAD]
        mine[j, 1] = normed[r : r + 16, c : c + HEAD]
        pair = fresh32[2 * j : 2 * j + 2, :]
        mine[j, 2] = jnp.concatenate([pair[:, :HEAD], pair[:, HEAD:], filler], axis=0).astype(BF16)
    row_copies = [
        to(mine.at[p], rows_got.at[me], rs1.at[k], rr1.at[k], section=p)
        for k, p in enumerate(partners)
    ]
    for copy in row_copies:
        copy.start()
    rows_got[me] = mine[me]

    turn(CHUNKS - 1)

    for copy in row_copies:
        copy.wait_recv()

    def pick_rows(p, _):
        rows_next[p] = rows_got[matching[p]]
        return 0

    lax.fori_loop(0, GROUPS, pick_rows, 0)
    row_copies2 = [
        to(rows_next.at[p], rows_out.at[me], rs2.at[k], rr2.at[k], section=p)
        for k, p in enumerate(partners)
    ]
    for copy in row_copies2:
        copy.start()
    rows_out[me] = rows_next[me]

    for i in range(3):
        for z2 in range(2):
            y_part(i, z2).wait_send()
    z_copy.wait_send()
    sq_copy.wait_send()
    for copy in sq_copies + row_copies:
        copy.wait_send()
    for q in range(CHUNKS):
        for k in range(PARTNERS):
            spread(q, k).wait_send()
    for q in range(CHUNKS):
        for copy in pass_on(q):
            copy.wait()
        leave(q).wait()
    for copy in row_copies2:
        copy.wait()


STEP = 4


def finish(lengths, moved, rows, cache_out, stream_out, normed_out):
    i = pl.program_id(0)

    @pl.when(i == 0)
    def _():
        for j in range(GROUPS):
            r, c = (j // 8) * 16, (j % 8) * HEAD
            stream_out[r : r + 16, c : c + HEAD] = rows[j, 0]
            normed_out[r : r + 16, c : c + HEAD] = rows[j, 1]

    place = lax.broadcasted_iota(jnp.int32, (SLOTS, HEAD), 0).astype(F32).astype(BF16)
    for b in range(STEP):
        new = rows[i * (STEP // 2) + b // 2, 2].astype(F32)
        here = place == lengths[i * STEP + b].astype(F32).astype(BF16)
        for half in range(2):
            row = 2 * half + b % 2
            new_row = jnp.broadcast_to(new[row : row + 1, :].astype(BF16), (SLOTS, HEAD))
            cols = slice(half * HEAD, (half + 1) * HEAD)
            cache_out[b, :, cols] = jnp.where(here, new_row, moved[b, :, cols])


def on_device(
    matching, lengths, queries, kv_cache, incoming_key_value, residual, out_weight, norm_gain
):
    smem = pl.BlockSpec(memory_space=pltpu.SMEM)
    vmem = pl.BlockSpec(memory_space=pltpu.VMEM)
    anywhere = pl.BlockSpec(memory_space=pl.ANY)
    chunk = pltpu.VMEM((GROUPS, 2, PER_CHUNK, 2 * HEAD), BF16)
    rows = pltpu.VMEM((GROUPS, 3, 16, HEAD), BF16)
    dma = pltpu.SemaphoreType.DMA
    moved, rows_moved = pl.pallas_call(
        kernel,
        out_shape=(
            jax.ShapeDtypeStruct((BATCH, SLOTS, 2 * HEAD), BF16),
            jax.ShapeDtypeStruct((GROUPS, 3, 16, HEAD), BF16),
        ),
        in_specs=[smem, smem, vmem, anywhere, vmem, vmem, anywhere, vmem],
        out_specs=(anywhere, vmem),
        scratch_shapes=[
            pltpu.VMEM((BATCH, SLOTS, 2 * HEAD), BF16),
            pltpu.VMEM((BATCH, 2 * HEAD), F32),
            pltpu.VMEM((BATCH * 8, HEAD), F32),
            pltpu.VMEM((BATCH * 8, HEAD), F32),
            pltpu.VMEM((8, 1024, 1024), BF16),
            pltpu.VMEM((8, BATCH, 1024), F32),
            pltpu.VMEM((3, 2, BATCH, 1024), F32),
            pltpu.VMEM((BATCH, 1024), F32),
            pltpu.VMEM((BATCH, 1024), F32),
            pltpu.VMEM((BATCH, HEAD), F32),
            pltpu.VMEM((3, BATCH, HEAD), F32),
            pltpu.VMEM((BATCH, HEAD), F32),
            pltpu.VMEM((BATCH, HEAD), F32),
            rows, rows, rows,
            [chunk] * CHUNKS,
            [chunk] * CHUNKS,
            dma, dma((8,)),
            dma((CHUNKS, PARTNERS)), dma((CHUNKS, PARTNERS)),
            dma((CHUNKS, PARTNERS)), dma((CHUNKS, PARTNERS)),
            dma((2, CHUNKS)),
            dma((3, 2)), dma((3, 2)), dma, dma,
            dma((3,)), dma((3,)), dma, dma,
            dma((PARTNERS,)), dma((PARTNERS,)), dma((PARTNERS,)), dma((PARTNERS,)),
        ],
        compiler_params=pltpu.CompilerParams(
            collective_id=0, has_side_effects=True, vmem_limit_bytes=56 << 20
        ),
    )(
        matching, lengths, queries[0], kv_cache[0], incoming_key_value[0],
        residual[0], out_weight[0], norm_gain,
    )
    whole = pl.BlockSpec((BATCH, 1024), lambda i: (0, 0))
    block = pl.BlockSpec((STEP, SLOTS, 2 * HEAD), lambda i: (i, 0, 0))
    cache_out, stream_out, normed_out = pl.pallas_call(
        finish,
        out_shape=(
            jax.ShapeDtypeStruct((BATCH, SLOTS, 2 * HEAD), BF16),
            jax.ShapeDtypeStruct((BATCH, 1024), BF16),
            jax.ShapeDtypeStruct((BATCH, 1024), BF16),
        ),
        grid=(BATCH // STEP,),
        in_specs=[smem, block, pl.BlockSpec((GROUPS, 3, 16, HEAD), lambda i: (0, 0, 0, 0))],
        out_specs=(block, whole, whole),
    )(lengths, moved, rows_moved)
    return cache_out[None], stream_out[None], normed_out[None]


def solution(mesh):
    return jax.shard_map(
        on_device,
        mesh=mesh,
        in_specs=(
            P(),
            P(),
            P("section", None, "tensor"),
            P("section", None, None, "tensor"),
            P("section", None, "tensor"),
            P("section", None, "tensor"),
            P("section", "tensor", None),
            P("section", "tensor"),
        ),
        out_specs=(
            P("section", None, None, "tensor"),
            P("section", None, "tensor"),
            P("section", None, "tensor"),
        ),
        check_vma=False,
    )
```

```python
import functools
import math

import jax
import jax.numpy as jnp
from jax import lax
from jax.experimental import pallas as pl
from jax.experimental.pallas import tpu as pltpu
from jax.sharding import PartitionSpec as P

MESH = pl.DeviceIdType.MESH
D = 8192
HEAD = 128
BATCH = 32
SLOTS = 256
GROUPS = 16
CHUNKS = 4
PER_CHUNK = SLOTS // CHUNKS
F32 = jnp.float32
BF16 = jnp.bfloat16

OFFSETS = []
for other_core in (0, 1):
    OFFSETS += [
        (1, 2, other_core), (0, 1, other_core), (1, 3, other_core), (0, 2, other_core),
        (1, 1, other_core), (0, 3, other_core), (1, 0, other_core),
    ]
OFFSETS += [(0, 0, 1)]
PARTNERS = len(OFFSETS)


def kernel(
    matching, lengths, queries_in, kv, fresh_in, residual_in, weight, gain_in,
    cache_out, rows_out, new_out,
    queries, fresh, residual, gain,
    cache, fresh32, asked, attended, wide, partial, y_got, z_part, z_got, stream32, squares, sq_got,
    mine, rows_got, rows_next, new_mine, new_got, new_next, got, nxt,
    small_sem, load_sem, weight_sem, send1, recv1, send2, recv2, own_sem,
    y_send, y_recv, z_send, z_recv, sq_send, sq_recv,
    rs1, rr1, rs2, rr2, ns1, nr1, ns2, nr2,
):
    me = lax.axis_index("section")
    zlo, x, core = me // 8, (me // 2) % 4, me % 2
    t = lax.axis_index("tensor")
    zhi, y = t // 4, t % 4
    partners = [
        ((zlo + dz) % 2) * 8 + ((x + dx) % 4) * 2 + (core + dc) % 2 for dz, dx, dc in OFFSETS
    ]
    y_partners = [zhi * 4 + (y + d) % 4 for d in (1, 2, 3)]
    z_partner = (1 - zhi) * 4 + y
    t_partners = y_partners + [z_partner] + [(1 - zhi) * 4 + (y + d) % 4 for d in (1, 2, 3)]

    def to(src, dst, ss, rs, **where):
        return pltpu.make_async_remote_copy(
            src, dst, ss, rs, device_id=where, device_id_type=MESH
        )

    barrier = pltpu.get_barrier_semaphore()
    for p in partners:
        pl.semaphore_signal(barrier, inc=1, device_id={"section": p}, device_id_type=MESH)
    for p in t_partners:
        pl.semaphore_signal(barrier, inc=1, device_id={"tensor": p}, device_id_type=MESH)

    load = pltpu.make_async_copy(kv, cache, load_sem)
    small = [
        pltpu.make_async_copy(src, dst, small_sem.at[i])
        for i, (src, dst) in enumerate(
            [(queries_in, queries), (fresh_in, fresh), (residual_in, residual), (gain_in, gain)]
        )
    ]
    for copy in small:
        copy.start()
    load.start()

    def block_of(n):
        return (n % 2) * 4 + (y + 1 + n // 2) % 4

    def load_weight(n):
        cols = pl.ds(pl.multiple_of(block_of(n) * 1024, 1024), 1024)
        return pltpu.make_async_copy(weight.at[:, cols], wide.at[n], weight_sem.at[n])

    def spread(q, k):
        p = partners[k]
        return to(
            kv.at[pl.ds(2 * p, 2), pl.ds(q * PER_CHUNK, PER_CHUNK)], got[q].at[me],
            send1.at[q, k], recv1.at[q, k], section=p,
        )

    def keep(q):
        return pltpu.make_async_copy(
            kv.at[pl.ds(2 * me, 2), pl.ds(q * PER_CHUNK, PER_CHUNK)], got[q].at[me],
            own_sem.at[0, q],
        )

    def spread_all(q):
        for k in range(PARTNERS):
            spread(q, k).start()
        keep(q).start()

    pl.semaphore_wait(barrier, PARTNERS + 7)
    spread_all(0)
    for copy in small:
        copy.wait()
    fresh32[...] = fresh[...].astype(F32)
    for j in range(GROUPS):
        pair = fresh32[2 * j : 2 * j + 2, :]
        new_mine[j] = jnp.concatenate([pair[:, :HEAD], pair[:, HEAD:]], axis=0).astype(BF16)
    new_copies = [
        to(new_mine.at[p], new_got.at[me], ns1.at[k], nr1.at[k], section=p)
        for k, p in enumerate(partners)
    ]
    for copy in new_copies:
        copy.start()
    new_got[me] = new_mine[me]
    for n in range(8):
        load_weight(n).start()
    for q in range(1, 3):
        spread_all(q)

    for h in range(8):
        asked[pl.ds(h, BATCH, stride=8), :] = queries[:, h * HEAD : (h + 1) * HEAD].astype(F32)
    load.wait()

    def attend(b):
        query = asked[pl.ds(pl.multiple_of(b * 8, 8), 8), :]
        keys, values = cache[b, :, :HEAD], cache[b, :, HEAD:]
        newest = fresh32[pl.ds(b, 1), :]
        new_key, new_value = newest[:, :HEAD], newest[:, HEAD:]
        scores = lax.dot_general(
            query.astype(BF16), keys, (((1,), (1,)), ((), ())), preferred_element_type=F32
        )
        place = lax.broadcasted_iota(jnp.int32, scores.shape, 1)
        own = jnp.sum(query * new_key, axis=1, keepdims=True)
        scores = jnp.where(place == lengths[b], own, scores) * (1.0 / math.sqrt(HEAD))
        scores = jnp.where(place <= lengths[b], scores, -1e30)
        grown = jnp.exp(scores - jnp.max(scores, axis=1, keepdims=True))
        weights = (grown / jnp.sum(grown, axis=1, keepdims=True)).astype(BF16).astype(F32)
        old = jnp.where(place == lengths[b], 0.0, weights)
        result = jnp.dot(old.astype(BF16), values, preferred_element_type=F32)
        result = result + jnp.sum(weights - old, axis=1, keepdims=True) * new_value
        attended[pl.ds(pl.multiple_of(b * 8, 8), 8), :] = result.astype(BF16).astype(F32)

    def attend_some(i, _):
        for j in range(4):
            attend(i * 4 + j)
        return 0

    lax.fori_loop(0, BATCH // 4, attend_some, 0)
    heads = jnp.concatenate(
        [attended[pl.ds(h, BATCH, stride=8), :].astype(BF16) for h in range(8)], axis=1
    )

    def y_part(i, z2):
        return to(
            partial.at[z2 * 4 + (y + 1 + i) % 4], y_got.at[i, z2],
            y_send.at[i, z2], y_recv.at[i, z2], tensor=y_partners[i],
        )

    for n in range(8):
        load_weight(n).wait()
        partial[block_of(n)] = jnp.dot(heads, wide[n], preferred_element_type=F32)
        if n < 6:
            y_part(n // 2, n % 2).start()

    def pass_on(q):
        return [
            to(
                nxt[q].at[partners[k]],
                cache_out.at[pl.ds(2 * me, 2), pl.ds(q * PER_CHUNK, PER_CHUNK)],
                send2.at[q, k], recv2.at[q, k], section=partners[k],
            )
            for k in range(PARTNERS)
        ]

    def leave(q):
        return pltpu.make_async_copy(
            nxt[q].at[me], cache_out.at[pl.ds(2 * me, 2), pl.ds(q * PER_CHUNK, PER_CHUNK)],
            own_sem.at[1, q],
        )

    def turn(q):
        keep(q).wait()
        for k in range(PARTNERS):
            spread(q, k).wait_recv()

        def pick(p, _):
            nxt[q][p] = got[q][matching[p]]
            return 0

        lax.fori_loop(0, GROUPS, pick, 0)
        for copy in pass_on(q):
            copy.start()
        leave(q).start()

    z_copy = to(z_part, z_got, z_send, z_recv, tensor=z_partner)
    sq_copies = [
        to(squares, sq_got.at[i], sq_send.at[i], sq_recv.at[i], tensor=p)
        for i, p in enumerate(t_partners)
    ]
    row_copies = [
        to(mine.at[p], rows_got.at[me], rs1.at[k], rr1.at[k], section=p)
        for k, p in enumerate(partners)
    ]
    row_copies2 = [
        to(rows_next.at[p], rows_out.at[me], rs2.at[k], rr2.at[k], section=p)
        for k, p in enumerate(partners)
    ]

    def sum_y():
        for i in range(3):
            for z2 in range(2):
                y_part(i, z2).wait_recv()
        other, own = 1 - zhi, zhi
        z_part[...] = partial[other * 4 + y] + (y_got[0, other] + y_got[1, other] + y_got[2, other])
        z_copy.start()
        stream32[...] = partial[own * 4 + y] + (y_got[0, own] + y_got[1, own] + y_got[2, own])

    def diagonal():
        shape = (BATCH, HEAD)
        return lax.broadcasted_iota(jnp.int32, shape, 0) == lax.broadcasted_iota(jnp.int32, shape, 1)

    def sum_z():
        z_copy.wait_recv()
        stream = stream32[...] + z_got[...] + residual[...].astype(F32)
        stream32[...] = stream
        sums = jnp.broadcast_to(jnp.sum(stream * stream, axis=1, keepdims=True), (BATCH, HEAD))
        line = jnp.sum(jnp.where(diagonal(), sums, 0.0), axis=0, keepdims=True)
        squares[...] = jnp.broadcast_to(line, squares.shape)
        for copy in sq_copies:
            copy.start()

    def norm():
        for copy in sq_copies:
            copy.wait_recv()
        line = squares[...]
        for i in range(7):
            line = line + sq_got[i]
        line = jnp.broadcast_to(line[:1], (BATCH, HEAD))
        total = jnp.sum(jnp.where(diagonal(), line, 0.0), axis=1, keepdims=True)
        scale = lax.rsqrt(total / D + 1e-05)
        normed = (stream32[...] * scale * gain[...].astype(F32)).astype(BF16)
        stream = stream32[...].astype(BF16)
        for j in range(GROUPS):
            r, c = (j // 8) * 16, (j % 8) * HEAD
            mine[j, 0] = stream[r : r + 16, c : c + HEAD]
            mine[j, 1] = normed[r : r + 16, c : c + HEAD]
        for copy in row_copies:
            copy.start()
        rows_got[me] = mine[me]

    new_copies2 = [
        to(new_next.at[p], new_out.at[me], ns2.at[k], nr2.at[k], section=p)
        for k, p in enumerate(partners)
    ]

    def turn_new():
        for copy in new_copies:
            copy.wait_recv()

        def pick_new(p, _):
            new_next[p] = new_got[matching[p]]
            return 0

        lax.fori_loop(0, GROUPS, pick_new, 0)
        for copy in new_copies2:
            copy.start()
        new_out[me] = new_next[me]

    def turn_rows():
        for copy in row_copies:
            copy.wait_recv()

        def pick_rows(p, _):
            rows_next[p] = rows_got[matching[p]]
            return 0

        lax.fori_loop(0, GROUPS, pick_rows, 0)
        for copy in row_copies2:
            copy.start()
        rows_out[me] = rows_next[me]

    sum_y()
    spread_all(3)
    turn(0)
    turn_new()
    sum_z()
    turn(1)
    norm()
    turn(2)
    turn_rows()
    turn(3)

    for i in range(3):
        for z2 in range(2):
            y_part(i, z2).wait_send()
    z_copy.wait_send()
    for copy in sq_copies + row_copies + new_copies:
        copy.wait_send()
    for q in range(CHUNKS):
        for k in range(PARTNERS):
            spread(q, k).wait_send()
    for q in range(CHUNKS):
        for copy in pass_on(q):
            copy.wait()
        leave(q).wait()
    for copy in row_copies2 + new_copies2:
        copy.wait()


STEP = 8


def finish(lengths, moved, rows, newest, cache_out, stream_out, normed_out):
    i = pl.program_id(0)

    @pl.when(i == 0)
    def _():
        for j in range(GROUPS):
            r, c = (j // 8) * 16, (j % 8) * HEAD
            stream_out[r : r + 16, c : c + HEAD] = rows[j, 0]
            normed_out[r : r + 16, c : c + HEAD] = rows[j, 1]

    place = lax.broadcasted_iota(jnp.int32, (SLOTS, HEAD), 0).astype(F32).astype(BF16)
    for b in range(STEP):
        new = newest[i * (STEP // 2) + b // 2].astype(F32)
        here = place == lengths[i * STEP + b].astype(F32).astype(BF16)
        for half in range(2):
            row = 2 * half + b % 2
            new_row = jnp.broadcast_to(new[row : row + 1, :].astype(BF16), (SLOTS, HEAD))
            cols = slice(half * HEAD, (half + 1) * HEAD)
            cache_out[b, :, cols] = jnp.where(here, new_row, moved[i * STEP + b, :, cols])


def on_device(
    matching, lengths, queries, kv_cache, incoming_key_value, residual, out_weight, norm_gain
):
    smem = pl.BlockSpec(memory_space=pltpu.SMEM)
    stay = lambda array: pltpu.with_memory_space_constraint(array, pltpu.HBM)
    vmem = pl.BlockSpec(memory_space=pltpu.VMEM)
    anywhere = pl.BlockSpec(memory_space=pl.ANY)
    hbm = pl.BlockSpec(memory_space=pltpu.HBM)
    chunk = pltpu.VMEM((GROUPS, 2, PER_CHUNK, 2 * HEAD), BF16)
    rows = pltpu.VMEM((GROUPS, 2, 16, HEAD), BF16)
    new = pltpu.VMEM((GROUPS, 4, HEAD), BF16)
    dma = pltpu.SemaphoreType.DMA
    moved, rows_moved, new_moved = pl.pallas_call(
        kernel,
        out_shape=(
            jax.ShapeDtypeStruct((BATCH, SLOTS, 2 * HEAD), BF16),
            jax.ShapeDtypeStruct((GROUPS, 2, 16, HEAD), BF16),
            jax.ShapeDtypeStruct((GROUPS, 4, HEAD), BF16),
        ),
        in_specs=[smem, smem] + [hbm] * 6,
        out_specs=(anywhere, vmem, vmem),
        scratch_shapes=[
            pltpu.VMEM((BATCH, 1024), BF16),
            pltpu.VMEM((BATCH, 2 * HEAD), BF16),
            pltpu.VMEM((BATCH, 1024), BF16),
            pltpu.VMEM((1, 1024), BF16),
            pltpu.VMEM((BATCH, SLOTS, 2 * HEAD), BF16),
            pltpu.VMEM((BATCH, 2 * HEAD), F32),
            pltpu.VMEM((BATCH * 8, HEAD), F32),
            pltpu.VMEM((BATCH * 8, HEAD), F32),
            pltpu.VMEM((8, 1024, 1024), BF16),
            pltpu.VMEM((8, BATCH, 1024), F32),
            pltpu.VMEM((3, 2, BATCH, 1024), F32),
            pltpu.VMEM((BATCH, 1024), F32),
            pltpu.VMEM((BATCH, 1024), F32),
            pltpu.VMEM((BATCH, 1024), F32),
            pltpu.VMEM((8, HEAD), F32),
            pltpu.VMEM((7, 8, HEAD), F32),
            rows, rows, rows, new, new, new,
            [chunk] * CHUNKS,
            [chunk] * CHUNKS,
            dma((4,)), dma, dma((8,)),
            dma((CHUNKS, PARTNERS)), dma((CHUNKS, PARTNERS)),
            dma((CHUNKS, PARTNERS)), dma((CHUNKS, PARTNERS)),
            dma((2, CHUNKS)),
            dma((3, 2)), dma((3, 2)), dma, dma, dma((7,)), dma((7,)),
            *([dma((PARTNERS,))] * 8),
        ],
        compiler_params=pltpu.CompilerParams(
            collective_id=0, has_side_effects=True, vmem_limit_bytes=34 << 20
        ),
    )(
        stay(matching), stay(lengths), stay(queries[0]), stay(kv_cache[0]),
        stay(incoming_key_value[0]), stay(residual[0]), stay(out_weight[0]), stay(norm_gain),
    )
    whole = pl.BlockSpec((BATCH, 1024), lambda i: (0, 0))
    block = pl.BlockSpec((STEP, SLOTS, 2 * HEAD), lambda i: (i, 0, 0))
    cache_out, stream_out, normed_out = pl.pallas_call(
        finish,
        out_shape=(
            jax.ShapeDtypeStruct((BATCH, SLOTS, 2 * HEAD), BF16),
            jax.ShapeDtypeStruct((BATCH, 1024), BF16),
            jax.ShapeDtypeStruct((BATCH, 1024), BF16),
        ),
        grid=(BATCH // STEP,),
        in_specs=[smem, vmem, vmem, vmem],
        out_specs=(block, whole, whole),
        compiler_params=pltpu.CompilerParams(vmem_limit_bytes=12 << 20),
    )(stay(lengths), moved, rows_moved, new_moved)
    return cache_out[None], stream_out[None], normed_out[None]


def solution(mesh):
    return jax.shard_map(
        on_device,
        mesh=mesh,
        in_specs=(
            P(),
            P(),
            P("section", None, "tensor"),
            P("section", None, None, "tensor"),
            P("section", None, "tensor"),
            P("section", None, "tensor"),
            P("section", "tensor", None),
            P("section", "tensor"),
        ),
        out_specs=(
            P("section", None, None, "tensor"),
            P("section", None, "tensor"),
            P("section", None, "tensor"),
        ),
        check_vma=False,
    )
```

```python
import functools
import math

import jax
import jax.numpy as jnp
from jax import lax
from jax.experimental import pallas as pl
from jax.experimental.pallas import tpu as pltpu
from jax.sharding import PartitionSpec as P

MESH = pl.DeviceIdType.MESH
D = 8192
HEAD = 128
BATCH = 32
SLOTS = 256
GROUPS = 16
CUTS = (96, 96, 64)
CHUNKS = len(CUTS)
F32 = jnp.float32
BF16 = jnp.bfloat16

OFFSETS = []
for other_core in (0, 1):
    OFFSETS += [
        (1, 2, other_core), (0, 1, other_core), (1, 3, other_core), (0, 2, other_core),
        (1, 1, other_core), (0, 3, other_core), (1, 0, other_core),
    ]
OFFSETS += [(0, 0, 1)]
PARTNERS = len(OFFSETS)


def slots(q):
    return slice(sum(CUTS[:q]), sum(CUTS[: q + 1]))


def kernel(
    matching, lengths, queries_in, kv, fresh_in, residual_in, weight, gain_in,
    cache_out, rows_out, new_out,
    queries, fresh, residual, gain,
    cache, fresh32, asked, attended, wide, partial, y_got, z_part, z_got, stream32, squares, sq_got,
    mine, rows_got, rows_next, new_mine, new_got, new_next, got, nxt,
    small_sem, load_sem, weight_sem, send1, recv1, send2, recv2, own_sem,
    y_send, y_recv, z_send, z_recv, sq_send, sq_recv,
    rs1, rr1, rs2, rr2, ns1, nr1, ns2, nr2,
):
    me = lax.axis_index("section")
    zlo, x, core = me // 8, (me // 2) % 4, me % 2
    t = lax.axis_index("tensor")
    zhi, y = t // 4, t % 4
    partners = [
        ((zlo + dz) % 2) * 8 + ((x + dx) % 4) * 2 + (core + dc) % 2 for dz, dx, dc in OFFSETS
    ]
    y_partners = [zhi * 4 + (y + d) % 4 for d in (1, 2, 3)]
    z_partner = (1 - zhi) * 4 + y
    t_partners = y_partners + [z_partner] + [(1 - zhi) * 4 + (y + d) % 4 for d in (1, 2, 3)]

    def to(src, dst, ss, rs, **where):
        return pltpu.make_async_remote_copy(
            src, dst, ss, rs, device_id=where, device_id_type=MESH
        )

    barrier = pltpu.get_barrier_semaphore()
    for p in partners:
        pl.semaphore_signal(barrier, inc=1, device_id={"section": p}, device_id_type=MESH)
    for p in t_partners:
        pl.semaphore_signal(barrier, inc=1, device_id={"tensor": p}, device_id_type=MESH)

    load = pltpu.make_async_copy(kv, cache, load_sem)
    small = [
        pltpu.make_async_copy(src, dst, small_sem.at[i])
        for i, (src, dst) in enumerate(
            [(queries_in, queries), (fresh_in, fresh), (residual_in, residual), (gain_in, gain)]
        )
    ]
    for copy in small:
        copy.start()
    load.start()

    def block_of(n):
        return (n % 2) * 4 + (y + 1 + n // 2) % 4

    def load_weight(n):
        cols = pl.ds(pl.multiple_of(block_of(n) * 1024, 1024), 1024)
        return pltpu.make_async_copy(weight.at[:, cols], wide.at[n], weight_sem.at[n])

    def spread(q, k):
        p = partners[k]
        return to(
            kv.at[pl.ds(2 * p, 2), slots(q)], got[q].at[me],
            send1.at[q, k], recv1.at[q, k], section=p,
        )

    def keep(q):
        return pltpu.make_async_copy(
            kv.at[pl.ds(2 * me, 2), slots(q)], got[q].at[me],
            own_sem.at[0, q],
        )

    def spread_all(q):
        for k in range(PARTNERS):
            spread(q, k).start()
        keep(q).start()

    pl.semaphore_wait(barrier, PARTNERS + 7)
    spread_all(0)
    for copy in small:
        copy.wait()
    fresh32[...] = fresh[...].astype(F32)
    for j in range(GROUPS):
        pair = fresh32[2 * j : 2 * j + 2, :]
        new_mine[j] = jnp.concatenate([pair[:, :HEAD], pair[:, HEAD:]], axis=0).astype(BF16)
    new_copies = [
        to(new_mine.at[p], new_got.at[me], ns1.at[k], nr1.at[k], section=p)
        for k, p in enumerate(partners)
    ]
    for copy in new_copies:
        copy.start()
    new_got[me] = new_mine[me]
    for n in range(8):
        load_weight(n).start()
    for q in range(1, 2):
        spread_all(q)

    for h in range(8):
        asked[pl.ds(h, BATCH, stride=8), :] = queries[:, h * HEAD : (h + 1) * HEAD].astype(F32)
    load.wait()

    def attend(b):
        query = asked[pl.ds(pl.multiple_of(b * 8, 8), 8), :]
        keys, values = cache[b, :, :HEAD], cache[b, :, HEAD:]
        newest = fresh32[pl.ds(b, 1), :]
        new_key, new_value = newest[:, :HEAD], newest[:, HEAD:]
        scores = lax.dot_general(
            query.astype(BF16), keys, (((1,), (1,)), ((), ())), preferred_element_type=F32
        )
        place = lax.broadcasted_iota(jnp.int32, scores.shape, 1)
        own = jnp.sum(query * new_key, axis=1, keepdims=True)
        scores = jnp.where(place == lengths[b], own, scores) * (1.0 / math.sqrt(HEAD))
        scores = jnp.where(place <= lengths[b], scores, -1e30)
        grown = jnp.exp(scores - jnp.max(scores, axis=1, keepdims=True))
        weights = (grown / jnp.sum(grown, axis=1, keepdims=True)).astype(BF16).astype(F32)
        old = jnp.where(place == lengths[b], 0.0, weights)
        result = jnp.dot(old.astype(BF16), values, preferred_element_type=F32)
        result = result + jnp.sum(weights - old, axis=1, keepdims=True) * new_value
        attended[pl.ds(pl.multiple_of(b * 8, 8), 8), :] = result.astype(BF16).astype(F32)

    def attend_some(i, _):
        for j in range(4):
            attend(i * 4 + j)
        return 0

    lax.fori_loop(0, BATCH // 4, attend_some, 0)
    heads = jnp.concatenate(
        [attended[pl.ds(h, BATCH, stride=8), :].astype(BF16) for h in range(8)], axis=1
    )

    def y_part(i, z2):
        return to(
            partial.at[z2 * 4 + (y + 1 + i) % 4], y_got.at[i, z2],
            y_send.at[i, z2], y_recv.at[i, z2], tensor=y_partners[i],
        )

    for n in range(8):
        load_weight(n).wait()
        partial[block_of(n)] = jnp.dot(heads, wide[n], preferred_element_type=F32)
        if n < 6:
            y_part(n // 2, n % 2).start()

    def pass_on(q):
        return [
            to(
                nxt[q].at[partners[k]],
                cache_out.at[pl.ds(2 * me, 2), slots(q)],
                send2.at[q, k], recv2.at[q, k], section=partners[k],
            )
            for k in range(PARTNERS)
        ]

    def leave(q):
        return pltpu.make_async_copy(
            nxt[q].at[me], cache_out.at[pl.ds(2 * me, 2), slots(q)],
            own_sem.at[1, q],
        )

    def turn(q):
        keep(q).wait()
        for k in range(PARTNERS):
            spread(q, k).wait_recv()

        def pick(p, _):
            nxt[q][p] = got[q][matching[p]]
            return 0

        lax.fori_loop(0, GROUPS, pick, 0)
        for copy in pass_on(q):
            copy.start()
        leave(q).start()

    z_copy = to(z_part, z_got, z_send, z_recv, tensor=z_partner)
    sq_copies = [
        to(squares, sq_got.at[i], sq_send.at[i], sq_recv.at[i], tensor=p)
        for i, p in enumerate(t_partners)
    ]
    row_copies = [
        to(mine.at[p], rows_got.at[me], rs1.at[k], rr1.at[k], section=p)
        for k, p in enumerate(partners)
    ]
    row_copies2 = [
        to(rows_next.at[p], rows_out.at[me], rs2.at[k], rr2.at[k], section=p)
        for k, p in enumerate(partners)
    ]

    def sum_y():
        for i in range(3):
            for z2 in range(2):
                y_part(i, z2).wait_recv()
        other, own = 1 - zhi, zhi
        half = partial[other * 4 + y] + (y_got[0, other] + y_got[1, other] + y_got[2, other])
        z_part[...] = half.astype(BF16)
        z_copy.start()
        stream32[...] = partial[own * 4 + y] + (y_got[0, own] + y_got[1, own] + y_got[2, own])

    def diagonal():
        shape = (BATCH, HEAD)
        return lax.broadcasted_iota(jnp.int32, shape, 0) == lax.broadcasted_iota(jnp.int32, shape, 1)

    def sum_z():
        z_copy.wait_recv()
        stream = stream32[...] + z_got[...].astype(F32) + residual[...].astype(F32)
        stream32[...] = stream
        sums = jnp.broadcast_to(jnp.sum(stream * stream, axis=1, keepdims=True), (BATCH, HEAD))
        line = jnp.sum(jnp.where(diagonal(), sums, 0.0), axis=0, keepdims=True)
        squares[...] = jnp.broadcast_to(line, squares.shape)
        for copy in sq_copies:
            copy.start()

    def norm():
        for copy in sq_copies:
            copy.wait_recv()
        line = squares[...]
        for i in range(7):
            line = line + sq_got[i]
        line = jnp.broadcast_to(line[:1], (BATCH, HEAD))
        total = jnp.sum(jnp.where(diagonal(), line, 0.0), axis=1, keepdims=True)
        scale = lax.rsqrt(total / D + 1e-05)
        normed = (stream32[...] * scale * gain[...].astype(F32)).astype(BF16)
        stream = stream32[...].astype(BF16)
        for j in range(GROUPS):
            r, c = (j // 8) * 16, (j % 8) * HEAD
            mine[j, 0] = stream[r : r + 16, c : c + HEAD]
            mine[j, 1] = normed[r : r + 16, c : c + HEAD]
        for copy in row_copies:
            copy.start()
        rows_got[me] = mine[me]

    new_copies2 = [
        to(new_next.at[p], new_out.at[me], ns2.at[k], nr2.at[k], section=p)
        for k, p in enumerate(partners)
    ]

    def turn_new():
        for copy in new_copies:
            copy.wait_recv()

        def pick_new(p, _):
            new_next[p] = new_got[matching[p]]
            return 0

        lax.fori_loop(0, GROUPS, pick_new, 0)
        for copy in new_copies2:
            copy.start()
        new_out[me] = new_next[me]

    def turn_rows():
        for copy in row_copies:
            copy.wait_recv()

        def pick_rows(p, _):
            rows_next[p] = rows_got[matching[p]]
            return 0

        lax.fori_loop(0, GROUPS, pick_rows, 0)
        for copy in row_copies2:
            copy.start()
        rows_out[me] = rows_next[me]

    sum_y()
    spread_all(2)
    turn_new()
    sum_z()
    turn(0)
    norm()
    turn(1)
    turn_rows()
    turn(2)

    for i in range(3):
        for z2 in range(2):
            y_part(i, z2).wait_send()
    z_copy.wait_send()
    for copy in sq_copies + row_copies + new_copies:
        copy.wait_send()
    for q in range(CHUNKS):
        for k in range(PARTNERS):
            spread(q, k).wait_send()
    for q in range(CHUNKS):
        for copy in pass_on(q):
            copy.wait()
        leave(q).wait()
    for copy in row_copies2 + new_copies2:
        copy.wait()


STEP = 2


def finish(
    lengths, moved, rows, newest, cache_out, stream_out, normed_out,
    cache, stream, normed, sems, row_sems,
):
    for j in range(GROUPS):
        r, c = (j // 8) * 16, (j % 8) * HEAD
        stream[r : r + 16, c : c + HEAD] = rows[j, 0]
        normed[r : r + 16, c : c + HEAD] = rows[j, 1]
    row_copies = [
        pltpu.make_async_copy(stream, stream_out, row_sems.at[0]),
        pltpu.make_async_copy(normed, normed_out, row_sems.at[1]),
    ]
    for copy in row_copies:
        copy.start()

    def store(i):
        part = pl.ds(i * STEP, STEP)
        return pltpu.make_async_copy(cache.at[part], cache_out.at[part], sems.at[i])

    place = lax.broadcasted_iota(jnp.int32, (SLOTS, HEAD), 0).astype(F32).astype(BF16)

    def write(i, _):
        for b in range(STEP):
            new = newest[i * (STEP // 2) + b // 2].astype(F32)
            here = place == lengths[i * STEP + b].astype(F32).astype(BF16)
            for half in range(2):
                row = 2 * half + b % 2
                new_row = jnp.broadcast_to(new[row : row + 1, :].astype(BF16), (SLOTS, HEAD))
                cols = slice(half * HEAD, (half + 1) * HEAD)
                cache[i * STEP + b, :, cols] = jnp.where(here, new_row, moved[i * STEP + b, :, cols])
        store(i).start()
        return 0

    lax.fori_loop(0, BATCH // STEP, write, 0)
    for i in range(BATCH // STEP):
        store(i).wait()
    for copy in row_copies:
        copy.wait()


def on_device(
    matching, lengths, queries, kv_cache, incoming_key_value, residual, out_weight, norm_gain
):
    smem = pl.BlockSpec(memory_space=pltpu.SMEM)
    stay = lambda array: pltpu.with_memory_space_constraint(array, pltpu.HBM)
    vmem = pl.BlockSpec(memory_space=pltpu.VMEM)
    anywhere = pl.BlockSpec(memory_space=pl.ANY)
    hbm = pl.BlockSpec(memory_space=pltpu.HBM)
    chunks = [pltpu.VMEM((GROUPS, 2, cut, 2 * HEAD), BF16) for cut in CUTS]
    rows = pltpu.VMEM((GROUPS, 2, 16, HEAD), BF16)
    new = pltpu.VMEM((GROUPS, 4, HEAD), BF16)
    dma = pltpu.SemaphoreType.DMA
    moved, rows_moved, new_moved = pl.pallas_call(
        kernel,
        out_shape=(
            jax.ShapeDtypeStruct((BATCH, SLOTS, 2 * HEAD), BF16),
            jax.ShapeDtypeStruct((GROUPS, 2, 16, HEAD), BF16),
            jax.ShapeDtypeStruct((GROUPS, 4, HEAD), BF16),
        ),
        in_specs=[smem, smem] + [hbm] * 6,
        out_specs=(anywhere, vmem, vmem),
        scratch_shapes=[
            pltpu.VMEM((BATCH, 1024), BF16),
            pltpu.VMEM((BATCH, 2 * HEAD), BF16),
            pltpu.VMEM((BATCH, 1024), BF16),
            pltpu.VMEM((1, 1024), BF16),
            pltpu.VMEM((BATCH, SLOTS, 2 * HEAD), BF16),
            pltpu.VMEM((BATCH, 2 * HEAD), F32),
            pltpu.VMEM((BATCH * 8, HEAD), F32),
            pltpu.VMEM((BATCH * 8, HEAD), F32),
            pltpu.VMEM((8, 1024, 1024), BF16),
            pltpu.VMEM((8, BATCH, 1024), F32),
            pltpu.VMEM((3, 2, BATCH, 1024), F32),
            pltpu.VMEM((BATCH, 1024), BF16),
            pltpu.VMEM((BATCH, 1024), BF16),
            pltpu.VMEM((BATCH, 1024), F32),
            pltpu.VMEM((8, HEAD), F32),
            pltpu.VMEM((7, 8, HEAD), F32),
            rows, rows, rows, new, new, new,
            chunks, chunks,
            dma((4,)), dma, dma((8,)),
            dma((CHUNKS, PARTNERS)), dma((CHUNKS, PARTNERS)),
            dma((CHUNKS, PARTNERS)), dma((CHUNKS, PARTNERS)),
            dma((2, CHUNKS)),
            dma((3, 2)), dma((3, 2)), dma, dma, dma((7,)), dma((7,)),
            *([dma((PARTNERS,))] * 8),
        ],
        compiler_params=pltpu.CompilerParams(
            collective_id=0, has_side_effects=True, vmem_limit_bytes=34 << 20
        ),
    )(
        stay(matching), stay(lengths), stay(queries[0]), stay(kv_cache[0]),
        stay(incoming_key_value[0]), stay(residual[0]), stay(out_weight[0]), stay(norm_gain),
    )
    cache_out, stream_out, normed_out = pl.pallas_call(
        finish,
        out_shape=(
            jax.ShapeDtypeStruct((BATCH, SLOTS, 2 * HEAD), BF16),
            jax.ShapeDtypeStruct((BATCH, 1024), BF16),
            jax.ShapeDtypeStruct((BATCH, 1024), BF16),
        ),
        in_specs=[smem, vmem, vmem, vmem],
        out_specs=(hbm, hbm, hbm),
        scratch_shapes=[
            pltpu.VMEM((BATCH, SLOTS, 2 * HEAD), BF16),
            pltpu.VMEM((BATCH, 1024), BF16),
            pltpu.VMEM((BATCH, 1024), BF16),
            dma((BATCH // STEP,)),
            dma((2,)),
        ],
        compiler_params=pltpu.CompilerParams(vmem_limit_bytes=12 << 20),
    )(stay(lengths), moved, rows_moved, new_moved)
    return cache_out[None], stream_out[None], normed_out[None]


def solution(mesh):
    return jax.shard_map(
        on_device,
        mesh=mesh,
        in_specs=(
            P(),
            P(),
            P("section", None, "tensor"),
            P("section", None, None, "tensor"),
            P("section", None, "tensor"),
            P("section", None, "tensor"),
            P("section", "tensor", None),
            P("section", "tensor"),
        ),
        out_specs=(
            P("section", None, None, "tensor"),
            P("section", None, "tensor"),
            P("section", None, "tensor"),
        ),
        check_vma=False,
    )
```

```python
import functools
import math

import jax
import jax.numpy as jnp
from jax import lax
from jax.experimental import pallas as pl
from jax.experimental.pallas import tpu as pltpu
from jax.sharding import PartitionSpec as P

MESH = pl.DeviceIdType.MESH
D = 8192
HEAD = 128
BATCH = 32
SLOTS = 256
GROUPS = 16
CUTS = (128, 80, 48)
CHUNKS = len(CUTS)
F32 = jnp.float32
BF16 = jnp.bfloat16

OFFSETS = []
for other_core in (0, 1):
    OFFSETS += [
        (1, 2, other_core), (0, 1, other_core), (1, 3, other_core), (0, 2, other_core),
        (1, 1, other_core), (0, 3, other_core), (1, 0, other_core),
    ]
OFFSETS += [(0, 0, 1)]
PARTNERS = len(OFFSETS)


def slots(q):
    return slice(sum(CUTS[:q]), sum(CUTS[: q + 1]))


def kernel(
    matching, lengths, queries_in, kv, fresh_in, residual_in, weight, gain_in,
    cache_out, rows_out,
    queries, fresh, residual, gain,
    cache, fresh32, asked, attended, wide, partial, y_got, z_part, z_got, stream32, squares, sq_got,
    mine, rows_got, rows_next, got, nxt,
    small_sem, load_sem, weight_sem, send1, recv1, send2, recv2, own_sem,
    y_send, y_recv, z_send, z_recv, sq_send, sq_recv,
    rs1, rr1, rs2, rr2,
):
    me = lax.axis_index("section")
    zlo, x, core = me // 8, (me // 2) % 4, me % 2
    t = lax.axis_index("tensor")
    zhi, y = t // 4, t % 4
    partners = [
        ((zlo + dz) % 2) * 8 + ((x + dx) % 4) * 2 + (core + dc) % 2 for dz, dx, dc in OFFSETS
    ]
    y_partners = [zhi * 4 + (y + d) % 4 for d in (1, 2, 3)]
    z_partner = (1 - zhi) * 4 + y
    t_partners = y_partners + [z_partner] + [(1 - zhi) * 4 + (y + d) % 4 for d in (1, 2, 3)]

    def to(src, dst, ss, rs, **where):
        return pltpu.make_async_remote_copy(
            src, dst, ss, rs, device_id=where, device_id_type=MESH
        )

    barrier = pltpu.get_barrier_semaphore()
    for p in partners:
        pl.semaphore_signal(barrier, inc=1, device_id={"section": p}, device_id_type=MESH)
    for p in t_partners:
        pl.semaphore_signal(barrier, inc=1, device_id={"tensor": p}, device_id_type=MESH)

    load = pltpu.make_async_copy(kv, cache, load_sem)
    small = [
        pltpu.make_async_copy(src, dst, small_sem.at[i])
        for i, (src, dst) in enumerate(
            [(queries_in, queries), (fresh_in, fresh), (residual_in, residual), (gain_in, gain)]
        )
    ]
    for copy in small:
        copy.start()
    load.start()

    def block_of(n):
        return (n % 2) * 4 + (y + 1 + n // 2) % 4

    def load_weight(n):
        cols = pl.ds(pl.multiple_of(block_of(n) * 1024, 1024), 1024)
        return pltpu.make_async_copy(weight.at[:, cols], wide.at[n], weight_sem.at[n])

    def spread(q, k):
        p = partners[k]
        return to(
            kv.at[pl.ds(2 * p, 2), slots(q)], got[q].at[me],
            send1.at[q, k], recv1.at[q, k], section=p,
        )

    def keep(q):
        return pltpu.make_async_copy(
            kv.at[pl.ds(2 * me, 2), slots(q)], got[q].at[me],
            own_sem.at[0, q],
        )

    def spread_all(q):
        for k in range(PARTNERS):
            spread(q, k).start()
        keep(q).start()

    pl.semaphore_wait(barrier, PARTNERS + 7)
    spread_all(0)
    for copy in small:
        copy.wait()
    fresh32[...] = fresh[...].astype(F32)
    for n in range(8):
        load_weight(n).start()
    for q in range(1, 2):
        spread_all(q)

    for h in range(8):
        asked[pl.ds(h, BATCH, stride=8), :] = queries[:, h * HEAD : (h + 1) * HEAD].astype(F32)
    load.wait()

    def attend(b):
        query = asked[pl.ds(pl.multiple_of(b * 8, 8), 8), :]
        keys, values = cache[b, :, :HEAD], cache[b, :, HEAD:]
        newest = fresh32[pl.ds(b, 1), :]
        new_key, new_value = newest[:, :HEAD], newest[:, HEAD:]
        scores = lax.dot_general(
            query.astype(BF16), keys, (((1,), (1,)), ((), ())), preferred_element_type=F32
        )
        place = lax.broadcasted_iota(jnp.int32, scores.shape, 1)
        own = jnp.sum(query * new_key, axis=1, keepdims=True)
        scores = jnp.where(place == lengths[b], own, scores) * (1.0 / math.sqrt(HEAD))
        scores = jnp.where(place <= lengths[b], scores, -1e30)
        grown = jnp.exp(scores - jnp.max(scores, axis=1, keepdims=True))
        weights = (grown / jnp.sum(grown, axis=1, keepdims=True)).astype(BF16).astype(F32)
        old = jnp.where(place == lengths[b], 0.0, weights)
        result = jnp.dot(old.astype(BF16), values, preferred_element_type=F32)
        result = result + jnp.sum(weights - old, axis=1, keepdims=True) * new_value
        attended[pl.ds(pl.multiple_of(b * 8, 8), 8), :] = result.astype(BF16).astype(F32)

    def attend_some(i, _):
        for j in range(4):
            attend(i * 4 + j)
        return 0

    lax.fori_loop(0, BATCH // 4, attend_some, 0)
    heads = jnp.concatenate(
        [attended[pl.ds(h, BATCH, stride=8), :].astype(BF16) for h in range(8)], axis=1
    )

    def y_part(i, z2):
        return to(
            partial.at[z2 * 4 + (y + 1 + i) % 4], y_got.at[i, z2],
            y_send.at[i, z2], y_recv.at[i, z2], tensor=y_partners[i],
        )

    for n in range(8):
        load_weight(n).wait()
        partial[block_of(n)] = jnp.dot(heads, wide[n], preferred_element_type=F32)
        if n < 6:
            y_part(n // 2, n % 2).start()

    def pass_on(q):
        return [
            to(
                nxt[q].at[partners[k]],
                cache_out.at[pl.ds(2 * me, 2), slots(q)],
                send2.at[q, k], recv2.at[q, k], section=partners[k],
            )
            for k in range(PARTNERS)
        ]

    def leave(q):
        return pltpu.make_async_copy(
            nxt[q].at[me], cache_out.at[pl.ds(2 * me, 2), slots(q)],
            own_sem.at[1, q],
        )

    def turn(q):
        keep(q).wait()
        for k in range(PARTNERS):
            spread(q, k).wait_recv()

        def pick(p, _):
            nxt[q][p] = got[q][matching[p]]
            return 0

        lax.fori_loop(0, GROUPS, pick, 0)
        for copy in pass_on(q):
            copy.start()
        leave(q).start()

    z_copy = to(z_part, z_got, z_send, z_recv, tensor=z_partner)
    sq_copies = [
        to(squares, sq_got.at[i], sq_send.at[i], sq_recv.at[i], tensor=p)
        for i, p in enumerate(t_partners)
    ]
    row_copies = [
        to(mine.at[p], rows_got.at[me], rs1.at[k], rr1.at[k], section=p)
        for k, p in enumerate(partners)
    ]
    row_copies2 = [
        to(rows_next.at[p], rows_out.at[me], rs2.at[k], rr2.at[k], section=p)
        for k, p in enumerate(partners)
    ]

    def sum_y():
        for i in range(3):
            for z2 in range(2):
                y_part(i, z2).wait_recv()
        other, own = 1 - zhi, zhi
        half = partial[other * 4 + y] + (y_got[0, other] + y_got[1, other] + y_got[2, other])
        z_part[...] = half.astype(BF16)
        z_copy.start()
        stream32[...] = partial[own * 4 + y] + (y_got[0, own] + y_got[1, own] + y_got[2, own])

    def diagonal():
        shape = (BATCH, HEAD)
        return lax.broadcasted_iota(jnp.int32, shape, 0) == lax.broadcasted_iota(jnp.int32, shape, 1)

    def sum_z():
        z_copy.wait_recv()
        stream = stream32[...] + z_got[...].astype(F32) + residual[...].astype(F32)
        stream32[...] = stream
        sums = jnp.broadcast_to(jnp.sum(stream * stream, axis=1, keepdims=True), (BATCH, HEAD))
        line = jnp.sum(jnp.where(diagonal(), sums, 0.0), axis=0, keepdims=True)
        squares[...] = jnp.broadcast_to(line, squares.shape)
        for copy in sq_copies:
            copy.start()

    def norm():
        for copy in sq_copies:
            copy.wait_recv()
        line = squares[...]
        for i in range(7):
            line = line + sq_got[i]
        line = jnp.broadcast_to(line[:1], (BATCH, HEAD))
        total = jnp.sum(jnp.where(diagonal(), line, 0.0), axis=1, keepdims=True)
        scale = lax.rsqrt(total / D + 1e-05)
        normed = (stream32[...] * scale * gain[...].astype(F32)).astype(BF16)
        stream = stream32[...].astype(BF16)
        for j in range(GROUPS):
            r, c = (j // 8) * 16, (j % 8) * HEAD
            mine[j, 0:16] = stream[r : r + 16, c : c + HEAD]
            mine[j, 16:32] = normed[r : r + 16, c : c + HEAD]
            pair = fresh32[2 * j : 2 * j + 2, :]
            both = jnp.concatenate([pair[:, :HEAD], pair[:, HEAD:]], axis=0)
            mine[j, 32:36] = both.astype(BF16)
        for copy in row_copies:
            copy.start()
        rows_got[me] = mine[me]

    def turn_rows():
        for copy in row_copies:
            copy.wait_recv()

        def pick_rows(p, _):
            rows_next[p] = rows_got[matching[p]]
            return 0

        lax.fori_loop(0, GROUPS, pick_rows, 0)
        for copy in row_copies2:
            copy.start()
        rows_out[me] = rows_next[me]

    sum_y()
    spread_all(2)
    sum_z()
    turn(0)
    norm()
    turn(1)
    turn_rows()
    turn(2)

    for i in range(3):
        for z2 in range(2):
            y_part(i, z2).wait_send()
    z_copy.wait_send()
    for copy in sq_copies + row_copies:
        copy.wait_send()
    for q in range(CHUNKS):
        for k in range(PARTNERS):
            spread(q, k).wait_send()
    for q in range(CHUNKS):
        for copy in pass_on(q):
            copy.wait()
        leave(q).wait()
    for copy in row_copies2:
        copy.wait()


STEP = 2


def finish(
    lengths, moved, rows, cache_out, stream_out, normed_out,
    cache, stream, normed, sems, row_sems,
):
    for j in range(GROUPS):
        r, c = (j // 8) * 16, (j % 8) * HEAD
        stream[r : r + 16, c : c + HEAD] = rows[j, 0:16]
        normed[r : r + 16, c : c + HEAD] = rows[j, 16:32]
    row_copies = [
        pltpu.make_async_copy(stream, stream_out, row_sems.at[0]),
        pltpu.make_async_copy(normed, normed_out, row_sems.at[1]),
    ]
    for copy in row_copies:
        copy.start()

    def store(i):
        part = pl.ds(i * STEP, STEP)
        return pltpu.make_async_copy(cache.at[part], cache_out.at[part], sems.at[i])

    place = lax.broadcasted_iota(jnp.int32, (SLOTS, HEAD), 0).astype(F32).astype(BF16)

    def write(i, _):
        for b in range(STEP):
            new = rows[i * (STEP // 2) + b // 2, 32:36].astype(F32)
            here = place == lengths[i * STEP + b].astype(F32).astype(BF16)
            for half in range(2):
                row = 2 * half + b % 2
                new_row = jnp.broadcast_to(new[row : row + 1, :].astype(BF16), (SLOTS, HEAD))
                cols = slice(half * HEAD, (half + 1) * HEAD)
                cache[i * STEP + b, :, cols] = jnp.where(here, new_row, moved[i * STEP + b, :, cols])
        store(i).start()
        return 0

    lax.fori_loop(0, BATCH // STEP, write, 0)
    for i in range(BATCH // STEP):
        store(i).wait()
    for copy in row_copies:
        copy.wait()


def on_device(
    matching, lengths, queries, kv_cache, incoming_key_value, residual, out_weight, norm_gain
):
    smem = pl.BlockSpec(memory_space=pltpu.SMEM)
    stay = lambda array: pltpu.with_memory_space_constraint(array, pltpu.HBM)
    vmem = pl.BlockSpec(memory_space=pltpu.VMEM)
    anywhere = pl.BlockSpec(memory_space=pl.ANY)
    hbm = pl.BlockSpec(memory_space=pltpu.HBM)
    chunks = [pltpu.VMEM((GROUPS, 2, cut, 2 * HEAD), BF16) for cut in CUTS]
    rows = pltpu.VMEM((GROUPS, 36, HEAD), BF16)
    dma = pltpu.SemaphoreType.DMA
    moved, rows_moved = pl.pallas_call(
        kernel,
        out_shape=(
            jax.ShapeDtypeStruct((BATCH, SLOTS, 2 * HEAD), BF16),
            jax.ShapeDtypeStruct((GROUPS, 36, HEAD), BF16),
        ),
        in_specs=[smem, smem] + [hbm] * 6,
        out_specs=(anywhere, vmem),
        scratch_shapes=[
            pltpu.VMEM((BATCH, 1024), BF16),
            pltpu.VMEM((BATCH, 2 * HEAD), BF16),
            pltpu.VMEM((BATCH, 1024), BF16),
            pltpu.VMEM((1, 1024), BF16),
            pltpu.VMEM((BATCH, SLOTS, 2 * HEAD), BF16),
            pltpu.VMEM((BATCH, 2 * HEAD), F32),
            pltpu.VMEM((BATCH * 8, HEAD), F32),
            pltpu.VMEM((BATCH * 8, HEAD), F32),
            pltpu.VMEM((8, 1024, 1024), BF16),
            pltpu.VMEM((8, BATCH, 1024), F32),
            pltpu.VMEM((3, 2, BATCH, 1024), F32),
            pltpu.VMEM((BATCH, 1024), BF16),
            pltpu.VMEM((BATCH, 1024), BF16),
            pltpu.VMEM((BATCH, 1024), F32),
            pltpu.VMEM((8, HEAD), F32),
            pltpu.VMEM((7, 8, HEAD), F32),
            rows, rows, rows,
            chunks, chunks,
            dma((4,)), dma, dma((8,)),
            dma((CHUNKS, PARTNERS)), dma((CHUNKS, PARTNERS)),
            dma((CHUNKS, PARTNERS)), dma((CHUNKS, PARTNERS)),
            dma((2, CHUNKS)),
            dma((3, 2)), dma((3, 2)), dma, dma, dma((7,)), dma((7,)),
            *([dma((PARTNERS,))] * 4),
        ],
        compiler_params=pltpu.CompilerParams(
            collective_id=0, has_side_effects=True, vmem_limit_bytes=34 << 20
        ),
    )(
        stay(matching), stay(lengths), stay(queries[0]), stay(kv_cache[0]),
        stay(incoming_key_value[0]), stay(residual[0]), stay(out_weight[0]), stay(norm_gain),
    )
    cache_out, stream_out, normed_out = pl.pallas_call(
        finish,
        out_shape=(
            jax.ShapeDtypeStruct((BATCH, SLOTS, 2 * HEAD), BF16),
            jax.ShapeDtypeStruct((BATCH, 1024), BF16),
            jax.ShapeDtypeStruct((BATCH, 1024), BF16),
        ),
        in_specs=[smem, vmem, vmem],
        out_specs=(hbm, hbm, hbm),
        scratch_shapes=[
            pltpu.VMEM((BATCH, SLOTS, 2 * HEAD), BF16),
            pltpu.VMEM((BATCH, 1024), BF16),
            pltpu.VMEM((BATCH, 1024), BF16),
            dma((BATCH // STEP,)),
            dma((2,)),
        ],
        compiler_params=pltpu.CompilerParams(vmem_limit_bytes=12 << 20),
    )(stay(lengths), moved, rows_moved)
    return cache_out[None], stream_out[None], normed_out[None]


def solution(mesh):
    return jax.shard_map(
        on_device,
        mesh=mesh,
        in_specs=(
            P(),
            P(),
            P("section", None, "tensor"),
            P("section", None, None, "tensor"),
            P("section", None, "tensor"),
            P("section", None, "tensor"),
            P("section", "tensor", None),
            P("section", "tensor"),
        ),
        out_specs=(
            P("section", None, None, "tensor"),
            P("section", None, "tensor"),
            P("section", None, "tensor"),
        ),
        check_vma=False,
    )
```

```python
import functools
import math

import jax
import jax.numpy as jnp
from jax import lax
from jax.experimental import pallas as pl
from jax.experimental.pallas import tpu as pltpu
from jax.sharding import PartitionSpec as P

MESH = pl.DeviceIdType.MESH
D = 8192
HEAD = 128
BATCH = 32
SLOTS = 256
GROUPS = 16
CUTS = (128, 80, 48)
CHUNKS = len(CUTS)
F32 = jnp.float32
BF16 = jnp.bfloat16

OFFSETS = []
for other_core in (0, 1):
    OFFSETS += [
        (1, 2, other_core), (0, 1, other_core), (1, 3, other_core), (0, 2, other_core),
        (1, 1, other_core), (0, 3, other_core), (1, 0, other_core),
    ]
OFFSETS += [(0, 0, 1)]
PARTNERS = len(OFFSETS)


def slots(q):
    return slice(sum(CUTS[:q]), sum(CUTS[: q + 1]))


def kernel(
    matching, lengths, queries_in, kv, fresh_in, residual_in, weight, gain_in,
    cache_out, rows_out,
    queries, fresh, residual, gain,
    cache, fresh32, asked, attended, wide, partial, y_got, z_part, z_got, stream32, squares, sq_got,
    mine, rows_got, rows_next, got, nxt,
    small_sem, load_sem, weight_sem, send1, recv1, send2, recv2, own_sem,
    y_send, y_recv, z_send, z_recv, sq_send, sq_recv,
    rs1, rr1, rs2, rr2,
):
    me = lax.axis_index("section")
    zlo, x, core = me // 8, (me // 2) % 4, me % 2
    t = lax.axis_index("tensor")
    zhi, y = t // 4, t % 4
    partners = [
        ((zlo + dz) % 2) * 8 + ((x + dx) % 4) * 2 + (core + dc) % 2 for dz, dx, dc in OFFSETS
    ]
    y_partners = [zhi * 4 + (y + d) % 4 for d in (1, 2, 3)]
    z_partner = (1 - zhi) * 4 + y
    t_partners = y_partners + [z_partner] + [(1 - zhi) * 4 + (y + d) % 4 for d in (1, 2, 3)]

    def to(src, dst, ss, rs, **where):
        return pltpu.make_async_remote_copy(
            src, dst, ss, rs, device_id=where, device_id_type=MESH
        )

    barrier = pltpu.get_barrier_semaphore()
    for p in partners:
        pl.semaphore_signal(barrier, inc=1, device_id={"section": p}, device_id_type=MESH)
    for p in t_partners:
        pl.semaphore_signal(barrier, inc=1, device_id={"tensor": p}, device_id_type=MESH)

    load = pltpu.make_async_copy(kv, cache, load_sem)
    small = [
        pltpu.make_async_copy(src, dst, small_sem.at[i])
        for i, (src, dst) in enumerate(
            [(queries_in, queries), (fresh_in, fresh), (residual_in, residual), (gain_in, gain)]
        )
    ]
    for copy in small:
        copy.start()
    load.start()

    def block_of(n):
        return (n % 2) * 4 + (y + 1 + n // 2) % 4

    def load_weight(n):
        cols = pl.ds(pl.multiple_of(block_of(n) * 1024, 1024), 1024)
        return pltpu.make_async_copy(weight.at[:, cols], wide.at[n], weight_sem.at[n])

    def spread(q, k):
        p = partners[k]
        return to(
            kv.at[pl.ds(2 * p, 2), slots(q)], got[q].at[me],
            send1.at[q, k], recv1.at[q, k], section=p,
        )

    def keep(q):
        return pltpu.make_async_copy(
            kv.at[pl.ds(2 * me, 2), slots(q)], got[q].at[me],
            own_sem.at[0, q],
        )

    def spread_all(q):
        for k in range(PARTNERS):
            spread(q, k).start()
        keep(q).start()

    pl.semaphore_wait(barrier, PARTNERS + 7)
    spread_all(0)
    for copy in small:
        copy.wait()
    fresh32[...] = fresh[...].astype(F32)
    for n in range(8):
        load_weight(n).start()
    for q in range(1, 2):
        spread_all(q)

    for h in range(8):
        asked[pl.ds(h, BATCH, stride=8), :] = queries[:, h * HEAD : (h + 1) * HEAD].astype(F32)
    load.wait()

    def attend(b):
        query = asked[pl.ds(pl.multiple_of(b * 8, 8), 8), :]
        keys, values = cache[b, :, :HEAD], cache[b, :, HEAD:]
        newest = fresh32[pl.ds(b, 1), :]
        new_key, new_value = newest[:, :HEAD], newest[:, HEAD:]
        scores = lax.dot_general(
            query.astype(BF16), keys, (((1,), (1,)), ((), ())), preferred_element_type=F32
        )
        place = lax.broadcasted_iota(jnp.int32, scores.shape, 1)
        own = jnp.sum(query * new_key, axis=1, keepdims=True)
        scores = jnp.where(place == lengths[b], own, scores) * (1.0 / math.sqrt(HEAD))
        scores = jnp.where(place <= lengths[b], scores, -1e30)
        grown = jnp.exp(scores - jnp.max(scores, axis=1, keepdims=True))
        weights = (grown / jnp.sum(grown, axis=1, keepdims=True)).astype(BF16).astype(F32)
        old = jnp.where(place == lengths[b], 0.0, weights)
        result = jnp.dot(old.astype(BF16), values, preferred_element_type=F32)
        result = result + jnp.sum(weights - old, axis=1, keepdims=True) * new_value
        attended[pl.ds(pl.multiple_of(b * 8, 8), 8), :] = result.astype(BF16).astype(F32)

    def attend_some(i, _):
        for j in range(4):
            attend(i * 4 + j)
        return 0

    lax.fori_loop(0, BATCH // 4, attend_some, 0)
    heads = jnp.concatenate(
        [attended[pl.ds(h, BATCH, stride=8), :].astype(BF16) for h in range(8)], axis=1
    )

    def y_part(i, z2):
        return to(
            partial.at[z2 * 4 + (y + 1 + i) % 4], y_got.at[i, z2],
            y_send.at[i, z2], y_recv.at[i, z2], tensor=y_partners[i],
        )

    for n in range(8):
        load_weight(n).wait()
        partial[block_of(n)] = jnp.dot(heads, wide[n], preferred_element_type=F32)
        if n < 6:
            y_part(n // 2, n % 2).start()

    def pass_on(q):
        return [
            to(
                nxt[q].at[partners[k]],
                cache_out.at[pl.ds(2 * me, 2), slots(q)],
                send2.at[q, k], recv2.at[q, k], section=partners[k],
            )
            for k in range(PARTNERS)
        ]

    def leave(q):
        return pltpu.make_async_copy(
            nxt[q].at[me], cache_out.at[pl.ds(2 * me, 2), slots(q)],
            own_sem.at[1, q],
        )

    def turn(q):
        keep(q).wait()
        for k in range(PARTNERS):
            spread(q, k).wait_recv()

        def pick(p, _):
            nxt[q][p] = got[q][matching[p]]
            return 0

        lax.fori_loop(0, GROUPS, pick, 0)
        for copy in pass_on(q)[::-1]:
            copy.start()
        leave(q).start()

    z_copy = to(z_part, z_got, z_send, z_recv, tensor=z_partner)
    sq_copies = [
        to(squares, sq_got.at[i], sq_send.at[i], sq_recv.at[i], tensor=p)
        for i, p in enumerate(t_partners)
    ]
    row_copies = [
        to(mine.at[p], rows_got.at[me], rs1.at[k], rr1.at[k], section=p)
        for k, p in enumerate(partners)
    ]
    row_copies2 = [
        to(rows_next.at[p], rows_out.at[me], rs2.at[k], rr2.at[k], section=p)
        for k, p in enumerate(partners)
    ]

    def sum_y():
        for i in range(3):
            for z2 in range(2):
                y_part(i, z2).wait_recv()
        other, own = 1 - zhi, zhi
        half = partial[other * 4 + y] + (y_got[0, other] + y_got[1, other] + y_got[2, other])
        z_part[...] = half.astype(BF16)
        z_copy.start()
        stream32[...] = partial[own * 4 + y] + (y_got[0, own] + y_got[1, own] + y_got[2, own])

    def diagonal():
        shape = (BATCH, HEAD)
        return lax.broadcasted_iota(jnp.int32, shape, 0) == lax.broadcasted_iota(jnp.int32, shape, 1)

    def sum_z():
        z_copy.wait_recv()
        stream = stream32[...] + z_got[...].astype(F32) + residual[...].astype(F32)
        stream32[...] = stream
        sums = jnp.broadcast_to(jnp.sum(stream * stream, axis=1, keepdims=True), (BATCH, HEAD))
        line = jnp.sum(jnp.where(diagonal(), sums, 0.0), axis=0, keepdims=True)
        squares[...] = jnp.broadcast_to(line, squares.shape)
        for copy in sq_copies:
            copy.start()

    def norm():
        for copy in sq_copies:
            copy.wait_recv()
        line = squares[...]
        for i in range(7):
            line = line + sq_got[i]
        line = jnp.broadcast_to(line[:1], (BATCH, HEAD))
        total = jnp.sum(jnp.where(diagonal(), line, 0.0), axis=1, keepdims=True)
        scale = lax.rsqrt(total / D + 1e-05)
        normed = (stream32[...] * scale * gain[...].astype(F32)).astype(BF16)
        stream = stream32[...].astype(BF16)
        for j in range(GROUPS):
            r, c = (j // 8) * 16, (j % 8) * HEAD
            mine[j, 0:16] = stream[r : r + 16, c : c + HEAD]
            mine[j, 16:32] = normed[r : r + 16, c : c + HEAD]
            pair = fresh32[2 * j : 2 * j + 2, :]
            both = jnp.concatenate([pair[:, :HEAD], pair[:, HEAD:]], axis=0)
            mine[j, 32:36] = both.astype(BF16)
        for copy in row_copies:
            copy.start()
        rows_got[me] = mine[me]

    def turn_rows():
        for copy in row_copies:
            copy.wait_recv()

        def pick_rows(p, _):
            rows_next[p] = rows_got[matching[p]]
            return 0

        lax.fori_loop(0, GROUPS, pick_rows, 0)
        for copy in row_copies2:
            copy.start()
        rows_out[me] = rows_next[me]

    sum_y()
    spread_all(2)
    sum_z()
    turn(0)
    norm()
    turn(1)
    turn_rows()
    turn(2)

    for i in range(3):
        for z2 in range(2):
            y_part(i, z2).wait_send()
    z_copy.wait_send()
    for copy in sq_copies + row_copies:
        copy.wait_send()
    for q in range(CHUNKS):
        for k in range(PARTNERS):
            spread(q, k).wait_send()
    for q in range(CHUNKS):
        for copy in pass_on(q):
            copy.wait()
        leave(q).wait()
    for copy in row_copies2:
        copy.wait()


STEP = 2


def finish(
    lengths, moved, rows, cache_out, stream_out, normed_out,
    cache, stream, normed, sems, row_sems,
):
    for j in range(GROUPS):
        r, c = (j // 8) * 16, (j % 8) * HEAD
        stream[r : r + 16, c : c + HEAD] = rows[j, 0:16]
        normed[r : r + 16, c : c + HEAD] = rows[j, 16:32]
    row_copies = [
        pltpu.make_async_copy(stream, stream_out, row_sems.at[0]),
        pltpu.make_async_copy(normed, normed_out, row_sems.at[1]),
    ]
    for copy in row_copies:
        copy.start()

    def store(i):
        part = pl.ds(i * STEP, STEP)
        return pltpu.make_async_copy(cache.at[part], cache_out.at[part], sems.at[i])

    place = lax.broadcasted_iota(jnp.int32, (SLOTS, HEAD), 0).astype(F32).astype(BF16)

    def write(i, _):
        for b in range(STEP):
            new = rows[i * (STEP // 2) + b // 2, 32:36].astype(F32)
            here = place == lengths[i * STEP + b].astype(F32).astype(BF16)
            for half in range(2):
                row = 2 * half + b % 2
                new_row = jnp.broadcast_to(new[row : row + 1, :].astype(BF16), (SLOTS, HEAD))
                cols = slice(half * HEAD, (half + 1) * HEAD)
                cache[i * STEP + b, :, cols] = jnp.where(here, new_row, moved[i * STEP + b, :, cols])
        store(i).start()
        return 0

    lax.fori_loop(0, BATCH // STEP, write, 0)
    for i in range(BATCH // STEP):
        store(i).wait()
    for copy in row_copies:
        copy.wait()


def on_device(
    matching, lengths, queries, kv_cache, incoming_key_value, residual, out_weight, norm_gain
):
    smem = pl.BlockSpec(memory_space=pltpu.SMEM)
    stay = lambda array: pltpu.with_memory_space_constraint(array, pltpu.HBM)
    vmem = pl.BlockSpec(memory_space=pltpu.VMEM)
    anywhere = pl.BlockSpec(memory_space=pl.ANY)
    hbm = pl.BlockSpec(memory_space=pltpu.HBM)
    chunks = [pltpu.VMEM((GROUPS, 2, cut, 2 * HEAD), BF16) for cut in CUTS]
    rows = pltpu.VMEM((GROUPS, 36, HEAD), BF16)
    dma = pltpu.SemaphoreType.DMA
    moved, rows_moved = pl.pallas_call(
        kernel,
        out_shape=(
            jax.ShapeDtypeStruct((BATCH, SLOTS, 2 * HEAD), BF16),
            jax.ShapeDtypeStruct((GROUPS, 36, HEAD), BF16),
        ),
        in_specs=[smem, smem] + [hbm] * 6,
        out_specs=(anywhere, vmem),
        scratch_shapes=[
            pltpu.VMEM((BATCH, 1024), BF16),
            pltpu.VMEM((BATCH, 2 * HEAD), BF16),
            pltpu.VMEM((BATCH, 1024), BF16),
            pltpu.VMEM((1, 1024), BF16),
            pltpu.VMEM((BATCH, SLOTS, 2 * HEAD), BF16),
            pltpu.VMEM((BATCH, 2 * HEAD), F32),
            pltpu.VMEM((BATCH * 8, HEAD), F32),
            pltpu.VMEM((BATCH * 8, HEAD), F32),
            pltpu.VMEM((8, 1024, 1024), BF16),
            pltpu.VMEM((8, BATCH, 1024), F32),
            pltpu.VMEM((3, 2, BATCH, 1024), F32),
            pltpu.VMEM((BATCH, 1024), BF16),
            pltpu.VMEM((BATCH, 1024), BF16),
            pltpu.VMEM((BATCH, 1024), F32),
            pltpu.VMEM((8, HEAD), F32),
            pltpu.VMEM((7, 8, HEAD), F32),
            rows, rows, rows,
            chunks, chunks,
            dma((4,)), dma, dma((8,)),
            dma((CHUNKS, PARTNERS)), dma((CHUNKS, PARTNERS)),
            dma((CHUNKS, PARTNERS)), dma((CHUNKS, PARTNERS)),
            dma((2, CHUNKS)),
            dma((3, 2)), dma((3, 2)), dma, dma, dma((7,)), dma((7,)),
            *([dma((PARTNERS,))] * 4),
        ],
        compiler_params=pltpu.CompilerParams(
            collective_id=0, has_side_effects=True, vmem_limit_bytes=34 << 20
        ),
    )(
        stay(matching), stay(lengths), stay(queries[0]), stay(kv_cache[0]),
        stay(incoming_key_value[0]), stay(residual[0]), stay(out_weight[0]), stay(norm_gain),
    )
    cache_out, stream_out, normed_out = pl.pallas_call(
        finish,
        out_shape=(
            jax.ShapeDtypeStruct((BATCH, SLOTS, 2 * HEAD), BF16),
            jax.ShapeDtypeStruct((BATCH, 1024), BF16),
            jax.ShapeDtypeStruct((BATCH, 1024), BF16),
        ),
        in_specs=[smem, vmem, vmem],
        out_specs=(hbm, hbm, hbm),
        scratch_shapes=[
            pltpu.VMEM((BATCH, SLOTS, 2 * HEAD), BF16),
            pltpu.VMEM((BATCH, 1024), BF16),
            pltpu.VMEM((BATCH, 1024), BF16),
            dma((BATCH // STEP,)),
            dma((2,)),
        ],
        compiler_params=pltpu.CompilerParams(vmem_limit_bytes=12 << 20),
    )(stay(lengths), moved, rows_moved)
    return cache_out[None], stream_out[None], normed_out[None]


def solution(mesh):
    return jax.shard_map(
        on_device,
        mesh=mesh,
        in_specs=(
            P(),
            P(),
            P("section", None, "tensor"),
            P("section", None, None, "tensor"),
            P("section", None, "tensor"),
            P("section", None, "tensor"),
            P("section", "tensor", None),
            P("section", "tensor"),
        ),
        out_specs=(
            P("section", None, None, "tensor"),
            P("section", None, "tensor"),
            P("section", None, "tensor"),
        ),
        check_vma=False,
    )
```
